32 devices in a mesh: dp: 8 (over z, y), fsdp: 4 (over x, core).
Axes of the slice: x: 2, y: 2, z: 4, core: 2. Of those that a mesh axis runs over, the one named last changes fastest.
Arguments:
- inputs: bfloat16 [28928, 768], P(('dp', 'fsdp')), may hold values from -6 to 6
- skip_input: bfloat16 [28928, 768], P(('dp', 'fsdp')), may hold values from -6 to 6
- cotangent: bfloat16 [28928, 768], P(('dp', 'fsdp')), may hold values from -6 to 6
- row_item: int32 [28928], P(('dp', 'fsdp')), may hold values from 0 to 2, as said below
- row_live: int32 [28928], P(('dp', 'fsdp')), may hold values from 0 to 1, as said below
- skip_weight: bfloat16 [768, 1536], P('fsdp'), may hold values from -0.15625 to 0.15625
- skip_bias: bfloat16 [768], P('fsdp'), may hold values from -1.5 to 1.5
- attn_gain: bfloat16 [768], P('fsdp'), may hold values from 0.099609375 to 1.8984375
- attn_shift: bfloat16 [768], P('fsdp'), may hold values from -1.5 to 1.5
- qkv_weight: bfloat16 [2304, 768], P('fsdp'), may hold values from -0.21875 to 0.21875
- proj_weight: bfloat16 [768, 768], P('fsdp'), may hold values from -3 to 3
- proj_bias: bfloat16 [768], P('fsdp'), may hold values from -1.5 to 1.5
- mlp_gain: bfloat16 [768], P('fsdp'), may hold values from 0.099609375 to 1.8984375
- mlp_shift: bfloat16 [768], P('fsdp'), may hold values from -1.5 to 1.5
- hidden_weight: bfloat16 [3072, 768], P('fsdp'), may hold values from -0.21875 to 0.21875
- hidden_bias: bfloat16 [3072], P('fsdp'), may hold values from -2.5 to 2.5
- output_weight: bfloat16 [768, 3072], P('fsdp'), may hold values from -0.109375 to 0.109375
- output_bias: bfloat16 [768], P('fsdp'), may hold values from -1.5 to 1.5
Outputs:
- output: bfloat16 [28928, 768], P(('dp', 'fsdp'))
- grad_input: bfloat16 [28928, 768], P(('dp', 'fsdp'))
- grad_skip: bfloat16 [28928, 768], P(('dp', 'fsdp'))
- grad_skip_weight: float32 [768, 1536], P('fsdp')
- grad_skip_bias: float32 [768], P('fsdp')
- grad_attn_gain: float32 [768], P('fsdp')
- grad_attn_shift: float32 [768], P('fsdp')
- grad_qkv_weight: float32 [2304, 768], P('fsdp')
- grad_proj_weight: float32 [768, 768], P('fsdp')
- grad_proj_bias: float32 [768], P('fsdp')
- grad_mlp_gain: float32 [768], P('fsdp')
- grad_mlp_shift: float32 [768], P('fsdp')
- grad_hidden_weight: float32 [3072, 768], P('fsdp')
- grad_hidden_bias: float32 [3072], P('fsdp')
- grad_output_weight: float32 [768, 3072], P('fsdp')
- grad_output_bias: float32 [768], P('fsdp')
The draws below stay inside these ranges and needn't reach their ends.
Inputs may be any that keep to these rules, and one draw needn't show every extreme that they name: `row_item`: each device's 904 rows hold, from its first row, either one item of 901 rows numbered 0, or 3 items of 257 rows numbered 0 to 2 in order; rows after the last item carry the last item's number. About a third of the devices hold one long item. `row_live`: 1 on the rows of items, 0 on the rows after them.
All inputs are finite; a program needn't handle non-finite values.
Results may differ from the reference program's by a relative error of at most 0.015.
Values may be sent and summed in bfloat16 or wider, within the bound.
No kernel may reach another device: no remote copies, remote signals or barrier semaphores. Data moves between devices by JAX's collectives and lax.ppermute only.
A program may use at most 192 MiB of HBM per device.

```python
import jax
import jax.numpy as jnp
from jax import lax

D = 768
H = 12
HD = 64
FF = 3072
SHORT = 257
LONG = 901
SLOTS = 3
ROWS_DEV = 904
TOKENS = 28928
N_DP = 8
N_FSDP = 4


def build_layout(key):
    device_count = TOKENS // ROWS_DEV
    order_ranks = jax.random.permutation(jax.random.fold_in(key, 41), device_count)
    long_count = max(1, device_count // 3)
    long_mask = order_ranks < long_count
    positions = jnp.arange(ROWS_DEV)
    short_item = jnp.minimum(positions // SHORT, SLOTS - 1)
    short_live = positions < SLOTS * SHORT
    long_live = positions < LONG
    item_table = jnp.where(long_mask[:, None], jnp.zeros_like(short_item)[None, :], short_item[None, :])
    live_table = jnp.where(long_mask[:, None], long_live[None, :], short_live[None, :])
    return (item_table.reshape(-1).astype(jnp.int32), live_table.reshape(-1).astype(jnp.int32))


def draw_row_item(key, part):
    return build_layout(key)[0]


def draw_row_live(key, part):
    return build_layout(key)[1]


def level_of(own_key, shape, cuts, least, largest):
    gain, own = 1.0, jax.random.fold_in(own_key, 6)
    for axis_at, blocks in cuts:
        steps = jnp.exp(jax.random.uniform(jax.random.fold_in(own, axis_at), (blocks,), jnp.float32, least / len(cuts), largest / len(cuts)))
        gain = gain * jnp.repeat(steps, shape[axis_at] // blocks).reshape([-1 if axis == axis_at else 1 for axis in range(len(shape))])
    return gain


def gaussian(key, shape, spread, bound, shards=(), dtype=jnp.bfloat16):
    factor_of = level_of(key, shape, shards, -0.22, 0.18) if shards else 1.0
    array = jax.random.normal(key, shape, jnp.float32) * spread * factor_of
    return jnp.minimum(jnp.maximum(array, -bound), bound).astype(dtype)


def setup_inputs(seed: int = 0) -> dict:
    arg_keys = jax.random.split(jax.random.key(seed), 19)
    inputs = gaussian(arg_keys[0], (TOKENS, D), 1.0, 6.0, ((0, 32),))
    skip_input = gaussian(arg_keys[1], (TOKENS, D), 1.0, 6.0, ((0, 32),))
    cotangent = gaussian(arg_keys[2], (TOKENS, D), 1.0, 6.0, ((0, 32),))
    row_item = draw_row_item(jax.random.fold_in(arg_keys[18], 71), 0)
    row_live = draw_row_live(jax.random.fold_in(arg_keys[18], 71), 0)
    skip_weight = gaussian(arg_keys[5], (D, 2 * D), (2 * D) ** -0.5, 0.15625, ((0, 4),))
    skip_bias = gaussian(arg_keys[6], (D,), 0.3, 1.5, ((0, 4),))
    attn_gain = jnp.clip(1.0 + 0.18 * jax.random.normal(arg_keys[7], (D,), jnp.float32), 0.099609375, 1.8984375).astype(jnp.bfloat16)
    attn_shift = gaussian(arg_keys[8], (D,), 0.3, 1.5, ((0, 4),))
    qkv_weight = gaussian(arg_keys[9], (3 * D, D), D ** -0.5, 0.21875, ((0, 4),))
    proj_weight = gaussian(arg_keys[10], (D, D), (max(4, 3 * D // ROWS_DEV)) ** -0.5, 3.0, ((0, 4),))
    proj_bias = gaussian(arg_keys[11], (D,), 0.3, 1.5, ((0, 4),))
    mlp_gain = jnp.clip(1.0 + 0.18 * jax.random.normal(arg_keys[12], (D,), jnp.float32), 0.099609375, 1.8984375).astype(jnp.bfloat16)
    mlp_shift = gaussian(arg_keys[13], (D,), 0.3, 1.5, ((0, 4),))
    hidden_weight = gaussian(arg_keys[14], (FF, D), D ** -0.5, 0.21875, ((0, 4),))
    hidden_bias = gaussian(arg_keys[15], (FF,), 0.5, 2.5, ((0, 4),))
    output_weight = gaussian(arg_keys[16], (D, FF), FF ** -0.5, 0.109375, ((0, 4),))
    output_bias = gaussian(arg_keys[17], (D,), 0.3, 1.5, ((0, 4),))
    return {"inputs": inputs, "skip_input": skip_input, "cotangent": cotangent, "row_item": row_item, "row_live": row_live, "skip_weight": skip_weight, "skip_bias": skip_bias, "attn_gain": attn_gain, "attn_shift": attn_shift, "qkv_weight": qkv_weight, "proj_weight": proj_weight, "proj_bias": proj_bias, "mlp_gain": mlp_gain, "mlp_shift": mlp_shift, "hidden_weight": hidden_weight, "hidden_bias": hidden_bias, "output_weight": output_weight, "output_bias": output_bias}


@jax.custom_vjp
def low(v):
    return lax.optimization_barrier(v.astype(jnp.bfloat16)).astype(jnp.float32)

@jax.custom_vjp
def low_back(v):
    return v

def low_keep(v):
    return (low(v), None)

def low_pass(kept, grad):
    return (grad,)

def back_keep(v):
    return (v, None)

def back_low(kept, grad):
    return (low(grad),)
low.defvjp(low_keep, low_pass)
low_back.defvjp(back_keep, back_low)
epsilon = 1e-05
masked_score = -1e+30

def layer_norm(stream, norm_gain, norm_shift):
    row_mean = lax.optimization_barrier(jnp.mean(stream, axis=1, keepdims=True))
    centred = stream - row_mean
    row_var = lax.optimization_barrier(jnp.mean(centred * centred, axis=1, keepdims=True))
    return centred * lax.rsqrt(row_var + epsilon) * norm_gain + norm_shift

def times_t(left, weight):
    return jnp.dot(left, weight.T, precision=lax.Precision.HIGHEST)

def forward(params, joined, row_item, row_live):
    skip_weight, skip_bias, attn_gain, attn_shift, qkv_weight, proj_weight, proj_bias, mlp_gain, mlp_shift, hidden_weight, hidden_bias, output_weight, output_bias = params
    row_count = joined.shape[0]
    stream_a = low_back(times_t(joined, skip_weight) + skip_bias)
    normed_a = low(layer_norm(stream_a, attn_gain, attn_shift))
    packed = low_back(low(times_t(normed_a, qkv_weight)))
    queries = packed[:, :D].reshape(row_count, H, HD)
    keys_all = packed[:, D:2 * D].reshape(row_count, H, HD)
    values_all = packed[:, 2 * D:].reshape(row_count, H, HD)
    scores = jnp.einsum('qhd,khd->hqk', queries, keys_all, precision=lax.Precision.HIGHEST)
    scores = low_back(scores * HD ** (-0.5))
    allowed = (row_item[:, None] == row_item[None, :]) & (row_live[None, :] == 1)
    scores = jnp.where(allowed[None], scores, masked_score)
    probs = low(jax.nn.softmax(scores, axis=-1))
    attended = jnp.einsum('hqk,khd->qhd', probs, values_all, precision=lax.Precision.HIGHEST)
    attended = low_back(low(attended.reshape(row_count, D)))
    stream_b = stream_a + low_back(times_t(attended, proj_weight) + proj_bias)
    normed_b = low(layer_norm(stream_b, mlp_gain, mlp_shift))
    pre_act = low_back(times_t(normed_b, hidden_weight) + hidden_bias)
    activation = low(jax.nn.gelu(pre_act, approximate=False))
    return stream_b + times_t(activation, output_weight) + output_bias

def reference(inputs, skip_input, cotangent, row_item, row_live, skip_weight, skip_bias, attn_gain, attn_shift, qkv_weight, proj_weight, proj_bias, mlp_gain, mlp_shift, hidden_weight, hidden_bias, output_weight, output_bias):
    params = tuple((member.astype(jnp.float32) for member in (skip_weight, skip_bias, attn_gain, attn_shift, qkv_weight, proj_weight, proj_bias, mlp_gain, mlp_shift, hidden_weight, hidden_bias, output_weight, output_bias)))
    device_total = N_DP * N_FSDP
    row_count = inputs.shape[0] // device_total
    joined = jnp.concatenate([inputs, skip_input], axis=1).astype(jnp.float32)
    joined = joined.reshape(device_total, row_count, 2 * D)
    cot_live = cotangent.astype(jnp.float32) * row_live[:, None].astype(jnp.float32)
    cot_live = cot_live.reshape(device_total, row_count, D)
    item_blocks = row_item.reshape(device_total, row_count)
    live_blocks = row_live.reshape(device_total, row_count)

    def one_block(totals, block):
        piece, items, lives, grad_piece = block
        result, back_fn = jax.vjp(lambda weights, rows: forward(weights, rows, items, lives), params, piece)
        grad_weights, grad_rows = back_fn(grad_piece)
        totals = jax.tree.map(lambda first, second: first + second, totals, grad_weights)
        return (totals, (result.astype(jnp.bfloat16), grad_rows.astype(jnp.bfloat16)))
    zero_grads = jax.tree.map(jnp.zeros_like, params)
    totals, (results, grad_rows) = lax.scan(one_block, zero_grads, (joined, item_blocks, live_blocks, cot_live))
    grads = [member / device_total for member in totals]
    output = results.reshape(-1, D)
    grad_input = grad_rows[:, :, :D].reshape(-1, D)
    grad_skip = grad_rows[:, :, D:].reshape(-1, D)
    return (output, grad_input, grad_skip, grads[0], grads[1], grads[2], grads[3], grads[4], grads[5], grads[6], grads[7], grads[8], grads[9], grads[10], grads[11], grads[12])
```

```python
import jax
import jax.numpy as jnp
from jax import lax
from jax.sharding import PartitionSpec as P

H = 12


epsilon = 1e-05
masked_score = -1e30


def layer_norm(stream, norm_gain, norm_shift):
    row_mean = jnp.mean(stream, axis=1, keepdims=True)
    centred = stream - row_mean
    row_var = jnp.mean(centred * centred, axis=1, keepdims=True)
    return centred * lax.rsqrt(row_var + epsilon) * norm_gain + norm_shift


def times_t(left, weight):
    return lax.dot_general(
        left, weight, (((1,), (1,)), ((), ())), preferred_element_type=jnp.float32
    )


def times_n(left, weight):
    return jnp.dot(left, weight, preferred_element_type=jnp.float32)


def rows_outer(grad_rows, left):
    return lax.dot_general(
        grad_rows, left, (((0,), (0,)), ((), ())), preferred_element_type=jnp.float32
    )


def column_sums(grad_rows):
    return jnp.sum(grad_rows.astype(jnp.float32), axis=0)


def bit_pairs(count, bit):
    return [(place, place ^ (1 << bit)) for place in range(count)]


def add_low(first, second):
    return (first.astype(jnp.float32) + second.astype(jnp.float32)).astype(jnp.bfloat16)


def half_swap(stack, axis_name, bit):
    mine = (lax.axis_index(axis_name) >> bit) & 1
    keep = lax.dynamic_index_in_dim(stack, mine, 1, keepdims=False)
    send = lax.dynamic_index_in_dim(stack, 1 - mine, 1, keepdims=False)
    return add_low(keep, lax.ppermute(send, axis_name, bit_pairs(lax.axis_size(axis_name), bit)))


def reduce_shard(grad):
    n_group, n_data = lax.axis_size("fsdp"), lax.axis_size("dp")
    rows, columns = grad.shape[0] // n_group, grad.shape[1]
    part = grad.reshape(n_group, rows, columns)
    for bit in range(n_group.bit_length() - 1):
        part = half_swap(part.reshape(-1, 2, rows, columns), "fsdp", bit)
    part = part.reshape(rows, columns)
    bits = n_data.bit_length() - 1
    for bit in range(bits - 1):
        part = half_swap(part.reshape(1, 2, -1, columns), "dp", bit)[0]
    part = add_low(part, lax.ppermute(part, "dp", bit_pairs(n_data, bits - 1)))
    for bit in reversed(range(bits - 1)):
        other = lax.ppermute(part, "dp", bit_pairs(n_data, bit))
        low = ((lax.axis_index("dp") >> bit) & 1) == 0
        part = jnp.where(
            low, jnp.concatenate([part, other], 0), jnp.concatenate([other, part], 0)
        )
    return part.astype(jnp.float32) / (n_group * n_data)


def shards(
    inputs,
    skip_input,
    cotangent,
    row_item,
    row_live,
    skip_weight,
    skip_bias,
    attn_gain,
    attn_shift,
    qkv_weight,
    proj_weight,
    proj_bias,
    mlp_gain,
    mlp_shift,
    hidden_weight,
    hidden_bias,
    output_weight,
    output_bias,
):
    row_count, model_width = inputs.shape
    head_size = model_width // H
    score_scale = head_size ** (-0.5)
    gathered = (
        lax.all_gather(skip_weight, "fsdp", axis=0, tiled=True),
        lax.all_gather(qkv_weight, "fsdp", axis=0, tiled=True),
        lax.all_gather(proj_weight, "fsdp", axis=0, tiled=True),
        lax.all_gather(skip_bias, "fsdp", axis=0, tiled=True),
        lax.all_gather(attn_gain, "fsdp", axis=0, tiled=True),
        lax.all_gather(attn_shift, "fsdp", axis=0, tiled=True),
        lax.all_gather(proj_bias, "fsdp", axis=0, tiled=True),
        lax.all_gather(mlp_gain, "fsdp", axis=0, tiled=True),
        lax.all_gather(mlp_shift, "fsdp", axis=0, tiled=True),
        lax.all_gather(hidden_bias, "fsdp", axis=0, tiled=True),
        lax.all_gather(output_bias, "fsdp", axis=0, tiled=True),
    )
    skip_full, qkv_full, proj_full = (gathered[0], gathered[1], gathered[2])
    (
        skip_vec,
        gain_first,
        shift_first,
        proj_vec,
        gain_second,
        shift_second,
        hidden_vec,
        output_vec,
    ) = [member.astype(jnp.float32) for member in gathered[3:]]
    joined = jnp.concatenate([inputs, skip_input], axis=1)
    stream_a = times_t(joined, skip_full) + skip_vec
    normed_a = layer_norm(stream_a, gain_first, shift_first).astype(jnp.bfloat16)
    packed = times_t(normed_a, qkv_full).astype(jnp.bfloat16)
    allowed = (row_item[:, None] == row_item[None, :]) & (row_live[None, :] == 1)

    def head_slices(head_index):
        query_head = lax.dynamic_slice_in_dim(packed, head_index * head_size, head_size, 1)
        key_head = lax.dynamic_slice_in_dim(
            packed, model_width + head_index * head_size, head_size, 1
        )
        value_head = lax.dynamic_slice_in_dim(
            packed, 2 * model_width + head_index * head_size, head_size, 1
        )
        scores = jnp.where(allowed, times_t(query_head, key_head) * score_scale, masked_score)
        return (query_head, key_head, value_head, scores)

    def head_forward(head_index, state):
        merged, log_totals = state
        query_head, key_head, value_head, scores = head_slices(head_index)
        row_max = jnp.max(scores, axis=1, keepdims=True)
        exp_scores = jnp.exp(scores - row_max)
        row_total = jnp.sum(exp_scores, axis=1, keepdims=True)
        attn_probs = (exp_scores / row_total).astype(jnp.bfloat16)
        head_out = times_n(attn_probs, value_head)
        merged = lax.dynamic_update_slice_in_dim(merged, head_out, head_index * head_size, 1)
        log_totals = lax.dynamic_update_slice_in_dim(
            log_totals, row_max + jnp.log(row_total), head_index, 1
        )
        return (merged, log_totals)

    merged, log_totals = lax.fori_loop(
        0,
        H,
        head_forward,
        (jnp.zeros((row_count, model_width), jnp.float32), jnp.zeros((row_count, H), jnp.float32)),
    )
    attended = merged.astype(jnp.bfloat16)
    stream_b = stream_a + times_t(attended, proj_full) + proj_vec
    normed_b = layer_norm(stream_b, gain_second, shift_second).astype(jnp.bfloat16)
    hidden_full, output_full = (
        lax.all_gather(hidden_weight, "fsdp", axis=0, tiled=True),
        lax.all_gather(output_weight, "fsdp", axis=0, tiled=True),
    )
    pre_act = times_t(normed_b, hidden_full) + hidden_vec
    activation = jax.nn.gelu(pre_act, approximate=False).astype(jnp.bfloat16)
    output = (stream_b + times_t(activation, output_full) + output_vec).astype(jnp.bfloat16)
    hidden_back, output_back = (hidden_full, output_full)
    grad_out = cotangent * row_live[:, None].astype(jnp.bfloat16)
    grad_output_weight = rows_outer(grad_out, activation)
    grad_output_bias = column_sums(grad_out)
    grad_act = times_n(grad_out, output_back)
    gelu_value, gelu_back = jax.vjp(lambda value: jax.nn.gelu(value, approximate=False), pre_act)
    grad_pre = gelu_back(grad_act)[0].astype(jnp.bfloat16)
    grad_hidden_weight = rows_outer(grad_pre, normed_b)
    grad_hidden_bias = column_sums(grad_pre)
    grad_normed_b = times_n(grad_pre, hidden_back)
    norm_value, norm_back = jax.vjp(layer_norm, stream_b, gain_second, shift_second)
    grad_part_b, grad_mlp_gain, grad_mlp_shift = norm_back(grad_normed_b)
    grad_stream_b = grad_out.astype(jnp.float32) + grad_part_b
    vec_grads = [grad_hidden_bias, grad_output_bias, grad_mlp_gain, grad_mlp_shift]
    final_hidden = reduce_shard(grad_hidden_weight.astype(jnp.bfloat16))
    final_output = reduce_shard(grad_output_weight.astype(jnp.bfloat16))
    skip_back, qkv_back, proj_back = (skip_full, qkv_full, proj_full)
    grad_branch = grad_stream_b.astype(jnp.bfloat16)
    grad_proj_weight = rows_outer(grad_branch, attended)
    grad_proj_bias = column_sums(grad_branch)
    grad_attended = times_n(grad_branch, proj_back).astype(jnp.bfloat16)

    def head_backward(head_index, grad_packed):
        query_head, key_head, value_head, scores = head_slices(head_index)
        log_head = lax.dynamic_slice_in_dim(log_totals, head_index, 1, 1)
        grad_head = lax.dynamic_slice_in_dim(grad_attended, head_index * head_size, head_size, 1)
        probs_full = jnp.exp(scores - log_head)
        grad_value = rows_outer(probs_full.astype(jnp.bfloat16), grad_head)
        grad_probs = times_t(grad_head, value_head)
        row_delta = jnp.sum(probs_full * grad_probs, axis=1, keepdims=True)
        grad_scores = (probs_full * (grad_probs - row_delta)).astype(jnp.bfloat16)
        grad_query = times_n(grad_scores, key_head) * score_scale
        grad_key = rows_outer(grad_scores, query_head) * score_scale
        grad_packed = lax.dynamic_update_slice_in_dim(
            grad_packed, grad_query, head_index * head_size, 1
        )
        grad_packed = lax.dynamic_update_slice_in_dim(
            grad_packed, grad_key, model_width + head_index * head_size, 1
        )
        grad_packed = lax.dynamic_update_slice_in_dim(
            grad_packed, grad_value, 2 * model_width + head_index * head_size, 1
        )
        return grad_packed

    grad_qkv = lax.fori_loop(
        0, H, head_backward, jnp.zeros((row_count, 3 * model_width), jnp.float32)
    ).astype(jnp.bfloat16)
    grad_qkv_weight = rows_outer(grad_qkv, normed_a)
    grad_normed_a = times_n(grad_qkv, qkv_back)
    first_value, first_back = jax.vjp(layer_norm, stream_a, gain_first, shift_first)
    grad_part_a, grad_attn_gain, grad_attn_shift = first_back(grad_normed_a)
    grad_rounded = (grad_stream_b + grad_part_a).astype(jnp.bfloat16)
    grad_skip_weight = rows_outer(grad_rounded, joined)
    grad_skip_bias = column_sums(grad_rounded)
    grad_joined = times_n(grad_rounded, skip_back)
    grad_input = grad_joined[:, :model_width].astype(jnp.bfloat16)
    grad_skip = grad_joined[:, model_width:].astype(jnp.bfloat16)
    final_proj = reduce_shard(grad_proj_weight.astype(jnp.bfloat16))
    final_qkv = reduce_shard(grad_qkv_weight.astype(jnp.bfloat16))
    n_group = lax.axis_size("fsdp")
    rows = model_width // n_group
    vectors = jnp.stack(
        [
            grad_skip_bias,
            grad_attn_gain,
            grad_attn_shift,
            grad_proj_bias,
            grad_mlp_gain,
            grad_mlp_shift,
            grad_output_bias,
        ]
    )
    wide = grad_hidden_bias.reshape(n_group, -1, rows)
    wide_count = wide.shape[1]
    wide = jnp.swapaxes(wide, 0, 1).reshape(wide_count, model_width)
    vectors = jnp.concatenate([vectors, wide], 0)
    vectors = jnp.pad(vectors, ((0, 128 - vectors.shape[0]), (0, 0))).T
    last = jnp.concatenate([grad_skip_weight, vectors], 1).astype(jnp.bfloat16)
    last = reduce_shard(last)
    final_skip = last[:, : 2 * model_width]
    final_vec = last[:, 2 * model_width :].T
    final_wide = final_vec[7 : 7 + wide_count].reshape(-1)
    return (
        output,
        grad_input,
        grad_skip,
        final_skip,
        final_vec[0],
        final_vec[1],
        final_vec[2],
        final_qkv,
        final_proj,
        final_vec[3],
        final_vec[4],
        final_vec[5],
        final_hidden,
        final_wide,
        final_output,
        final_vec[6],
    )


def solution(mesh):
    in_specs = (
        P(("dp", "fsdp"), None),
        P(("dp", "fsdp"), None),
        P(("dp", "fsdp"), None),
        P(("dp", "fsdp")),
        P(("dp", "fsdp")),
        P("fsdp", None),
        P("fsdp"),
        P("fsdp"),
        P("fsdp"),
        P("fsdp", None),
        P("fsdp", None),
        P("fsdp"),
        P("fsdp"),
        P("fsdp"),
        P("fsdp", None),
        P("fsdp"),
        P("fsdp", None),
        P("fsdp"),
    )
    out_specs = (
        P(("dp", "fsdp"), None),
        P(("dp", "fsdp"), None),
        P(("dp", "fsdp"), None),
        P("fsdp", None),
        P("fsdp"),
        P("fsdp"),
        P("fsdp"),
        P("fsdp", None),
        P("fsdp", None),
        P("fsdp"),
        P("fsdp"),
        P("fsdp"),
        P("fsdp", None),
        P("fsdp"),
        P("fsdp", None),
        P("fsdp"),
    )
    return jax.shard_map(shards, mesh=mesh, in_specs=in_specs, out_specs=out_specs, check_vma=False)
```

```python
import functools

import jax
import jax.numpy as jnp
from jax import lax
from jax.experimental import pallas as pl
from jax.experimental.pallas import tpu as pltpu
from jax.sharding import PartitionSpec as P

H = 12


epsilon = 1e-05
masked_score = -1e30


def layer_norm(stream, norm_gain, norm_shift):
    row_mean = jnp.mean(stream, axis=1, keepdims=True)
    centred = stream - row_mean
    row_var = jnp.mean(centred * centred, axis=1, keepdims=True)
    return centred * lax.rsqrt(row_var + epsilon) * norm_gain + norm_shift


def times_t(left, weight):
    return lax.dot_general(
        left, weight, (((1,), (1,)), ((), ())), preferred_element_type=jnp.float32
    )


def times_n(left, weight):
    return jnp.dot(left, weight, preferred_element_type=jnp.float32)


def rows_outer(grad_rows, left):
    return lax.dot_general(
        grad_rows, left, (((0,), (0,)), ((), ())), preferred_element_type=jnp.float32
    )


def column_sums(grad_rows):
    return jnp.sum(grad_rows.astype(jnp.float32), axis=0)


def bit_pairs(count, bit):
    return [(place, place ^ (1 << bit)) for place in range(count)]


def add_low(first, second):
    return (first.astype(jnp.float32) + second.astype(jnp.float32)).astype(jnp.bfloat16)


def half_swap(stack, axis_name, bit):
    mine = (lax.axis_index(axis_name) >> bit) & 1
    keep = lax.dynamic_index_in_dim(stack, mine, 1, keepdims=False)
    send = lax.dynamic_index_in_dim(stack, 1 - mine, 1, keepdims=False)
    return add_low(keep, lax.ppermute(send, axis_name, bit_pairs(lax.axis_size(axis_name), bit)))


def reduce_shard(grad):
    n_group, n_data = lax.axis_size("fsdp"), lax.axis_size("dp")
    rows, columns = grad.shape[0] // n_group, grad.shape[1]
    part = grad.reshape(n_group, rows, columns)
    for bit in range(n_group.bit_length() - 1):
        part = half_swap(part.reshape(-1, 2, rows, columns), "fsdp", bit)
    part = part.reshape(rows, columns)
    bits = n_data.bit_length() - 1
    for bit in range(bits - 1):
        part = half_swap(part.reshape(1, 2, -1, columns), "dp", bit)[0]
    part = add_low(part, lax.ppermute(part, "dp", bit_pairs(n_data, bits - 1)))
    for bit in reversed(range(bits - 1)):
        other = lax.ppermute(part, "dp", bit_pairs(n_data, bit))
        low = ((lax.axis_index("dp") >> bit) & 1) == 0
        part = jnp.where(
            low, jnp.concatenate([part, other], 0), jnp.concatenate([other, part], 0)
        )
    return part.astype(jnp.float32) / (n_group * n_data)


LANES = 128
f32, bf16 = jnp.float32, jnp.bfloat16
NT = (((1,), (1,)), ((), ()))
NN = (((1,), (0,)), ((), ()))


def dot_nt(left, right):
    return lax.dot_general(left, right, NT, preferred_element_type=f32)


def dot_nn(left, right):
    return lax.dot_general(left, right, NN, preferred_element_type=f32)


def lane_index(rows):
    return lax.broadcasted_iota(jnp.int32, (rows, LANES), 1)


def split_three(column, lane, rest):
    high = column.astype(bf16).astype(f32)
    middle = (column - high).astype(bf16).astype(f32)
    low = column - high - middle
    wide = jnp.where(lane == 3, high, jnp.where(lane == 4, middle, jnp.where(lane == 5, low, rest)))
    return wide.astype(bf16)


def padded(count, step):
    return -(-count // step) * step


def attention_forward_kernel(scale, rows, chunk, q_ref, k_ref, v_ref, qmark_ref, kmark_ref, out_ref, qaug_ref, qa, ka, va):
    total = qa.shape[0]
    keys = ka.shape[1]
    head = q_ref.shape[1] // 2
    qa[0:rows, 0:LANES] = q_ref[...] * jnp.asarray(scale, bf16)
    qa[0:rows, LANES:] = qmark_ref[...]
    lane_k = lane_index(rows)
    for j in range(2):
        own = (lane_k >= head * j) & (lane_k < head * (j + 1))
        k_own = jnp.where(own, k_ref[...], jnp.zeros_like(k_ref))
        ka[j, 0:rows, 0:LANES] = k_own
        ka[j, 0:rows, LANES:] = kmark_ref[...]
        ones = jnp.where(lane_k == head * (1 - j), jnp.ones_like(v_ref), jnp.zeros_like(v_ref))
        va[j, 0:rows, :] = jnp.where(own, v_ref[...], ones)
        va[j, rows:, :] = jnp.zeros((keys - rows, LANES), bf16)
        ka[j, rows:, 0:LANES] = jnp.zeros((keys - rows, LANES), bf16)
        lane_pad = lane_index(keys - rows)
        ka[j, rows:, LANES:] = jnp.where(lane_pad < 3, masked_score, 0.0).astype(bf16)
    if total > rows:
        lane_pad = lane_index(total - rows)
        qa[rows:, 0:LANES] = jnp.zeros((total - rows, LANES), bf16)
        qa[rows:, LANES:] = jnp.where(lane_pad == 0, 1.0, 0.0).astype(bf16)
    lane = lane_index(chunk)
    for start in range(0, total, chunk):
        q_rows = qa[start : start + chunk, :]
        outs = []
        size = min(chunk, rows - start)
        for j in range(2):
            scores = dot_nt(q_rows, ka[j])
            row_max = jnp.max(scores, axis=1, keepdims=True)
            probs = jnp.exp(scores - row_max).astype(bf16)
            out = dot_nn(probs, va[j])
            row_sum = out[:, head * (1 - j) : head * (1 - j) + 1]
            outs.append(out / row_sum)
            log_total = row_max + jnp.log(row_sum)
            aug = split_three(-log_total, lane, q_rows[:, LANES:].astype(f32))
            qaug_ref[start : start + size, j * LANES : (j + 1) * LANES] = aug[:size]
        both = jnp.where(lane < head, outs[0], outs[1]).astype(bf16)
        out_ref[start : start + size, :] = both[:size]


def attention_forward(packed, qmark, kmark, chunk=304):
    rows, width = packed.shape[0], packed.shape[1] // 3
    pairs = width // LANES
    total, keys = padded(rows, 16), padded(rows, 256)
    if total % chunk:
        chunk = total
    kernel = functools.partial(attention_forward_kernel, (width // H) ** (-0.5), rows, chunk)
    block = lambda offset: pl.BlockSpec((rows, LANES), lambda g: (0, g + offset))
    fixed = pl.BlockSpec((rows, LANES), lambda g: (0, 0))
    return pl.pallas_call(
        kernel,
        grid=(pairs,),
        in_specs=[block(0), block(pairs), block(2 * pairs), fixed, fixed],
        out_specs=[pl.BlockSpec((rows, LANES), lambda g: (0, g)), pl.BlockSpec((rows, 2 * LANES), lambda g: (0, g))],
        out_shape=[
            jax.ShapeDtypeStruct((rows, width), bf16),
            jax.ShapeDtypeStruct((rows, 2 * width), bf16),
        ],
        scratch_shapes=[
            pltpu.VMEM((total, 2 * LANES), bf16),
            pltpu.VMEM((2, keys, 2 * LANES), bf16),
            pltpu.VMEM((2, keys, LANES), bf16),
        ],
        name="attention_forward",
    )(packed, packed, packed, qmark, kmark)


def attention_backward_kernel(scale, rows, chunk, q_ref, k_ref, v_ref, go_ref, out_ref, qaug_ref, kmark_ref, dq_ref, dk_ref, dv_ref, qa, da, ka, va, kt, dqt):
    queries = qa.shape[1]
    total = ka.shape[0]
    head = q_ref.shape[1] // 2
    lane = lane_index(rows)
    ka[0:rows, 0:LANES] = k_ref[...]
    ka[0:rows, LANES:] = kmark_ref[...]
    va[0:rows, 0:LANES] = v_ref[...]
    ones = jnp.where((lane >= 3) & (lane < 6), 1.0, 0.0).astype(bf16)
    va[0:rows, LANES:] = ones
    if total > rows:
        pad = total - rows
        ka[rows:, 0:LANES] = jnp.zeros((pad, LANES), bf16)
        ka[rows:, LANES:] = jnp.where(lane_index(pad) < 3, masked_score, 0.0).astype(bf16)
        va[rows:, :] = jnp.zeros((pad, 2 * LANES), bf16)
    kt[...] = ka[:, 0:LANES].astype(f32).T.astype(bf16)
    for j in range(2):
        own = (lane >= head * j) & (lane < head * (j + 1))
        qa[j, 0:rows, 0:LANES] = jnp.where(own, q_ref[...] * jnp.asarray(scale, bf16), jnp.zeros_like(q_ref))
        qa[j, 0:rows, LANES:] = qaug_ref[:, j * LANES : (j + 1) * LANES]
        go = jnp.where(own, go_ref[...], jnp.zeros_like(go_ref))
        delta = jnp.sum(go.astype(f32) * out_ref[...].astype(f32), axis=1, keepdims=True)
        da[j, 0:rows, 0:LANES] = go
        da[j, 0:rows, LANES:] = split_three(-delta, lane, 0.0)
        qa[j, rows:, :] = jnp.zeros((queries - rows, 2 * LANES), bf16)
        da[j, rows:, :] = jnp.zeros((queries - rows, 2 * LANES), bf16)
    for start in range(0, total, chunk):
        here = slice(start, start + chunk)
        dk = dv = None
        size = min(chunk, rows - start)
        for j in range(2):
            probs = jnp.exp(dot_nt(ka[here, :], qa[j]))
            grad_probs = dot_nt(va[here, :], da[j])
            grad_scores = (probs * grad_probs).astype(bf16)
            dv_part = dot_nn(probs.astype(bf16), da[j, :, 0:LANES])
            dk_part = dot_nn(grad_scores, qa[j, :, 0:LANES])
            dq_part = dot_nn(kt[j * head : (j + 1) * head, here], grad_scores)
            spot = slice(j * head, (j + 1) * head)
            dqt[spot, :] = dq_part if start == 0 else dqt[spot, :] + dq_part
            dk = dk_part if dk is None else dk + dk_part
            dv = dv_part if dv is None else dv + dv_part
        dk_ref[start : start + size, :] = dk.astype(bf16)[:size]
        dv_ref[start : start + size, :] = dv.astype(bf16)[:size]
    dq_ref[...] = (dqt[...].T * scale).astype(bf16)[:rows]


def attention_backward(packed, grad_attended, attended, qaug, kmark, chunk=912):
    rows, width = packed.shape[0], packed.shape[1] // 3
    pairs = width // LANES
    queries = padded(rows, 256)
    total = padded(rows, 16)
    if total % chunk:
        chunk = total
    kernel = functools.partial(attention_backward_kernel, (width // H) ** (-0.5), rows, chunk)
    block = lambda offset: pl.BlockSpec((rows, LANES), lambda g: (0, g + offset))
    fixed = pl.BlockSpec((rows, LANES), lambda g: (0, 0))
    return pl.pallas_call(
        kernel,
        grid=(pairs,),
        in_specs=[block(0), block(pairs), block(2 * pairs), block(0), block(0), pl.BlockSpec((rows, 2 * LANES), lambda g: (0, g)), fixed],
        out_specs=[block(0)] * 3,
        out_shape=[jax.ShapeDtypeStruct((rows, width), bf16)] * 3,
        scratch_shapes=[
            pltpu.VMEM((2, queries, 2 * LANES), bf16),
            pltpu.VMEM((2, queries, 2 * LANES), bf16),
            pltpu.VMEM((total, 2 * LANES), bf16),
            pltpu.VMEM((total, 2 * LANES), bf16),
            pltpu.VMEM((LANES, total), bf16),
            pltpu.VMEM((LANES, queries), f32),
        ],
        name="attention_backward",
    )(packed, packed, packed, grad_attended, attended, qaug, kmark)


def marks(row_item, row_live):
    rows = row_item.shape[0]
    lane = lane_index(rows)
    item = row_item[:, None] == lane
    qmark = item.astype(bf16)
    barred = (lane < 3) & ~(item & (row_live[:, None] == 1))
    kmark = jnp.where(barred, masked_score, jnp.where((lane >= 3) & (lane < 6), 1.0, 0.0)).astype(bf16)
    return qmark, kmark


def place_kernel(half, place_ref, own, near, far, own_c, near_c, far_c, out_ref, sems):
    f, low = place_ref[0], place_ref[1]
    copies = []
    for at, (base, piece_own, piece_near, piece_far) in enumerate(
        ((f, own, near, far), (f ^ 1, own_c, near_c, far_c))
    ):
        begin = 2 * half * (base ^ 2)
        spots = (
            (piece_own, 2 * half * base, 2 * half),
            (piece_near, begin + half * low, half),
            (piece_far, begin + half * (1 - low), half),
        )
        for spot, (piece, start, size) in enumerate(spots):
            rows = pl.ds(pl.multiple_of(start, half), size)
            copies.append(
                pltpu.make_async_copy(piece, out_ref.at[rows, :], sems.at[3 * at + spot])
            )
    for copy in copies:
        copy.start()
    for copy in copies:
        copy.wait()


def gather_rows(shard, name):
    rows, columns = shard.shape
    half = rows // 2
    n_group, n_data = lax.axis_size("fsdp"), lax.axis_size("dp")
    low = lax.axis_index("dp") & 1
    send = lax.dynamic_slice_in_dim(shard, half * low, half, 0)
    near = lax.ppermute(send, "fsdp", bit_pairs(n_group, 1))
    own_c = lax.ppermute(shard, "fsdp", bit_pairs(n_group, 0))
    far = lax.ppermute(near, "dp", bit_pairs(n_data, 0))
    near_c = lax.ppermute(near, "fsdp", bit_pairs(n_group, 0))
    far_c = lax.ppermute(far, "fsdp", bit_pairs(n_group, 0))
    place = jnp.stack([lax.axis_index("fsdp"), low]).astype(jnp.int32)
    anywhere = pl.BlockSpec(memory_space=pl.ANY)
    return pl.pallas_call(
        functools.partial(place_kernel, half),
        in_specs=[pl.BlockSpec(memory_space=pltpu.SMEM)] + [anywhere] * 6,
        out_specs=pl.BlockSpec(memory_space=pltpu.VMEM),
        out_shape=jax.ShapeDtypeStruct((n_group * rows, columns), shard.dtype),
        scratch_shapes=[pltpu.SemaphoreType.DMA((6,))],
        name=name,
    )(place, shard, near, far, own_c, near_c, far_c)


def gather_vectors(members):
    n_group = lax.axis_size("fsdp")
    f = lax.axis_index("fsdp")
    joined = jnp.concatenate(members)[None, :]
    pair = lax.ppermute(joined, "fsdp", bit_pairs(n_group, 1))
    both = jnp.concatenate([joined, pair], 0)
    core = lax.ppermute(both, "fsdp", bit_pairs(n_group, 0))
    every = jnp.concatenate([both, core], 0)
    found = [every[0:1], every[2:3], every[1:2], every[3:4]]
    ordered = jnp.concatenate(
        [
            sum(
                jnp.where((f ^ at) == away, found[away], jnp.zeros_like(joined))
                for away in range(n_group)
            )
            for at in range(n_group)
        ],
        0,
    ).astype(jnp.float32)
    outs, start = [], 0
    for member in members:
        outs.append(ordered[:, start : start + member.shape[0]].reshape(-1))
        start += member.shape[0]
    return outs


def shards(
    inputs,
    skip_input,
    cotangent,
    row_item,
    row_live,
    skip_weight,
    skip_bias,
    attn_gain,
    attn_shift,
    qkv_weight,
    proj_weight,
    proj_bias,
    mlp_gain,
    mlp_shift,
    hidden_weight,
    hidden_bias,
    output_weight,
    output_bias,
):
    model_width = inputs.shape[1]
    skip_full = gather_rows(skip_weight, "place_skip")
    (
        skip_vec,
        gain_first,
        shift_first,
        proj_vec,
        gain_second,
        shift_second,
        hidden_vec,
        output_vec,
    ) = gather_vectors(
        [
            skip_bias,
            attn_gain,
            attn_shift,
            proj_bias,
            mlp_gain,
            mlp_shift,
            hidden_bias,
            output_bias,
        ]
    )
    qkv_full = gather_rows(qkv_weight, "place_qkv")
    proj_full = gather_rows(proj_weight, "place_proj")
    hidden_full = gather_rows(hidden_weight, "place_hidden")
    output_full = gather_rows(output_weight, "place_output")
    joined = jnp.concatenate([inputs, skip_input], axis=1)
    stream_a = times_t(joined, skip_full) + skip_vec
    normed_a = layer_norm(stream_a, gain_first, shift_first).astype(jnp.bfloat16)
    packed = times_t(normed_a, qkv_full).astype(jnp.bfloat16)
    qmark, kmark = marks(row_item, row_live)
    attended, qaug = attention_forward(packed, qmark, kmark)
    stream_b = stream_a + times_t(attended, proj_full) + proj_vec
    normed_b = layer_norm(stream_b, gain_second, shift_second).astype(jnp.bfloat16)
    pre_act = times_t(normed_b, hidden_full) + hidden_vec
    activation = jax.nn.gelu(pre_act, approximate=False).astype(jnp.bfloat16)
    output = (stream_b + times_t(activation, output_full) + output_vec).astype(jnp.bfloat16)
    hidden_back, output_back = (hidden_full, output_full)
    grad_out = cotangent * row_live[:, None].astype(jnp.bfloat16)
    grad_output_weight = rows_outer(grad_out, activation)
    grad_output_bias = column_sums(grad_out)
    grad_act = times_n(grad_out, output_back)
    gelu_value, gelu_back = jax.vjp(lambda value: jax.nn.gelu(value, approximate=False), pre_act)
    grad_pre = gelu_back(grad_act)[0].astype(jnp.bfloat16)
    grad_hidden_weight = rows_outer(grad_pre, normed_b)
    grad_hidden_bias = column_sums(grad_pre)
    grad_normed_b = times_n(grad_pre, hidden_back)
    norm_value, norm_back = jax.vjp(layer_norm, stream_b, gain_second, shift_second)
    grad_part_b, grad_mlp_gain, grad_mlp_shift = norm_back(grad_normed_b)
    grad_stream_b = grad_out.astype(jnp.float32) + grad_part_b
    vec_grads = [grad_hidden_bias, grad_output_bias, grad_mlp_gain, grad_mlp_shift]
    final_hidden = reduce_shard(grad_hidden_weight.astype(jnp.bfloat16))
    final_output = reduce_shard(grad_output_weight.astype(jnp.bfloat16))
    skip_back, qkv_back, proj_back = (skip_full, qkv_full, proj_full)
    grad_branch = grad_stream_b.astype(jnp.bfloat16)
    grad_proj_weight = rows_outer(grad_branch, attended)
    grad_proj_bias = column_sums(grad_branch)
    grad_attended = times_n(grad_branch, proj_back).astype(jnp.bfloat16)

    grad_qkv = jnp.concatenate(
        attention_backward(packed, grad_attended, attended, qaug, kmark), axis=1
    )
    grad_qkv_weight = rows_outer(grad_qkv, normed_a)
    grad_normed_a = times_n(grad_qkv, qkv_back)
    first_value, first_back = jax.vjp(layer_norm, stream_a, gain_first, shift_first)
    grad_part_a, grad_attn_gain, grad_attn_shift = first_back(grad_normed_a)
    grad_rounded = (grad_stream_b + grad_part_a).astype(jnp.bfloat16)
    grad_skip_weight = rows_outer(grad_rounded, joined)
    grad_skip_bias = column_sums(grad_rounded)
    grad_joined = times_n(grad_rounded, skip_back)
    grad_input = grad_joined[:, :model_width].astype(jnp.bfloat16)
    grad_skip = grad_joined[:, model_width:].astype(jnp.bfloat16)
    final_proj = reduce_shard(grad_proj_weight.astype(jnp.bfloat16))
    final_qkv = reduce_shard(grad_qkv_weight.astype(jnp.bfloat16))
    n_group = lax.axis_size("fsdp")
    rows = model_width // n_group
    vectors = jnp.stack(
        [
            grad_skip_bias,
            grad_attn_gain,
            grad_attn_shift,
            grad_proj_bias,
            grad_mlp_gain,
            grad_mlp_shift,
            grad_output_bias,
        ]
    )
    wide = grad_hidden_bias.reshape(n_group, -1, rows)
    wide_count = wide.shape[1]
    wide = jnp.swapaxes(wide, 0, 1).reshape(wide_count, model_width)
    vectors = jnp.concatenate([vectors, wide], 0)
    vectors = jnp.pad(vectors, ((0, 128 - vectors.shape[0]), (0, 0))).T
    last = jnp.concatenate([grad_skip_weight, vectors], 1).astype(jnp.bfloat16)
    last = reduce_shard(last)
    final_skip = last[:, : 2 * model_width]
    final_vec = last[:, 2 * model_width :].T
    final_wide = final_vec[7 : 7 + wide_count].reshape(-1)
    return (
        output,
        grad_input,
        grad_skip,
        final_skip,
        final_vec[0],
        final_vec[1],
        final_vec[2],
        final_qkv,
        final_proj,
        final_vec[3],
        final_vec[4],
        final_vec[5],
        final_hidden,
        final_wide,
        final_output,
        final_vec[6],
    )


def solution(mesh):
    in_specs = (
        P(("dp", "fsdp"), None),
        P(("dp", "fsdp"), None),
        P(("dp", "fsdp"), None),
        P(("dp", "fsdp")),
        P(("dp", "fsdp")),
        P("fsdp", None),
        P("fsdp"),
        P("fsdp"),
        P("fsdp"),
        P("fsdp", None),
        P("fsdp", None),
        P("fsdp"),
        P("fsdp"),
        P("fsdp"),
        P("fsdp", None),
        P("fsdp"),
        P("fsdp", None),
        P("fsdp"),
    )
    out_specs = (
        P(("dp", "fsdp"), None),
        P(("dp", "fsdp"), None),
        P(("dp", "fsdp"), None),
        P("fsdp", None),
        P("fsdp"),
        P("fsdp"),
        P("fsdp"),
        P("fsdp", None),
        P("fsdp", None),
        P("fsdp"),
        P("fsdp"),
        P("fsdp"),
        P("fsdp", None),
        P("fsdp"),
        P("fsdp", None),
        P("fsdp"),
    )
    return jax.shard_map(shards, mesh=mesh, in_specs=in_specs, out_specs=out_specs, check_vma=False)
```

```python
import functools

import jax
import jax.numpy as jnp
from jax import lax
from jax.experimental import pallas as pl
from jax.experimental.pallas import tpu as pltpu
from jax.sharding import PartitionSpec as P

H = 12


epsilon = 1e-05
masked_score = -1e30


def layer_norm(stream, norm_gain, norm_shift):
    row_mean = jnp.mean(stream, axis=1, keepdims=True)
    centred = stream - row_mean
    row_var = jnp.mean(centred * centred, axis=1, keepdims=True)
    return centred * lax.rsqrt(row_var + epsilon) * norm_gain + norm_shift


def times_t(left, weight):
    return lax.dot_general(
        left, weight, (((1,), (1,)), ((), ())), preferred_element_type=jnp.float32
    )


def times_n(left, weight):
    return jnp.dot(left, weight, preferred_element_type=jnp.float32)


def rows_outer(grad_rows, left):
    return lax.dot_general(
        grad_rows, left, (((0,), (0,)), ((), ())), preferred_element_type=jnp.float32
    )


def column_sums(grad_rows):
    return jnp.sum(grad_rows.astype(jnp.float32), axis=0)


def bit_pairs(count, bit):
    return [(place, place ^ (1 << bit)) for place in range(count)]


def add_low(first, second):
    return (first.astype(jnp.float32) + second.astype(jnp.float32)).astype(jnp.bfloat16)


def after(value, *gates):
    return lax.optimization_barrier((value,) + gates)[0]


class Reducer:
    def __init__(self, name, *grads):
        self.name = name
        self.n_group, self.n_data = lax.axis_size("fsdp"), lax.axis_size("dp")
        columns = grads[0].shape[1]
        self.parts = [grad.reshape(self.n_group, -1, columns) for grad in grads]
        bits = self.n_data.bit_length() - 1
        self.plan = [("fsdp", bit, "halve") for bit in range(self.n_group.bit_length() - 1)]
        self.plan += [("dp", bit, "halve") for bit in range(bits - 1)]
        self.plan += [("dp", bits - 1, "swap")]
        self.plan += [("dp", bit, "join") for bit in reversed(range(bits - 1))]
        self.flight = None
        self.at = 0

    def take(self, gates):
        if self.flight is None:
            return
        got = after(self.flight, *gates)
        axis, bit, kind = self.plan[self.at - 1]
        if kind == "join":
            low = ((lax.axis_index(axis) >> bit) & 1) == 0
            part = self.parts[0]
            part = jnp.where(
                low, jnp.concatenate([part, got], 1), jnp.concatenate([got, part], 1)
            )
        else:
            part = add_low(self.keep, got)
        self.parts = [part]

    def step(self, *gates):
        if self.at == len(self.plan):
            return self.parts[0]
        self.take(gates)
        axis, bit, kind = self.plan[self.at]
        self.at += 1
        if kind == "halve":
            mine = (lax.axis_index(axis) >> bit) & 1
            keeps, sends = [], []
            for part in self.parts:
                columns = part.shape[-1]
                if axis == "fsdp":
                    stack = part.reshape(part.shape[0] // 2, 2, -1, columns)
                else:
                    stack = part.reshape(1, 2, -1, columns)
                keeps.append(lax.dynamic_index_in_dim(stack, mine, 1, keepdims=False))
                sends.append(lax.dynamic_index_in_dim(stack, 1 - mine, 1, keepdims=False))
            self.keep = keeps[0] if len(keeps) == 1 else jnp.concatenate(keeps, 1)
            send = sends[0] if len(sends) == 1 else jnp.concatenate(sends, 1)
        else:
            send = self.keep = self.parts[0]
        with jax.named_scope(f"{self.name}_{self.at}"):
            self.flight = lax.ppermute(send, axis, bit_pairs(lax.axis_size(axis), bit))
        return send

    def finish(self, *gates):
        while self.at < len(self.plan):
            self.step(*gates)
        self.take(gates)
        return self.parts[0][0].astype(jnp.float32) / (self.n_group * self.n_data)


LANES = 128
f32, bf16 = jnp.float32, jnp.bfloat16
NT = (((1,), (1,)), ((), ()))
NN = (((1,), (0,)), ((), ()))


def dot_nt(left, right):
    return lax.dot_general(left, right, NT, preferred_element_type=f32)


def dot_nn(left, right):
    return lax.dot_general(left, right, NN, preferred_element_type=f32)


def lane_index(rows):
    return lax.broadcasted_iota(jnp.int32, (rows, LANES), 1)


def split_three(column, lane, rest):
    high = column.astype(bf16).astype(f32)
    middle = (column - high).astype(bf16).astype(f32)
    low = column - high - middle
    wide = jnp.where(lane == 3, high, jnp.where(lane == 4, middle, jnp.where(lane == 5, low, rest)))
    return wide.astype(bf16)


def padded(count, step):
    return -(-count // step) * step


def attention_forward_kernel(scale, rows, chunk, q_ref, k_ref, v_ref, qmark_ref, kmark_ref, out_ref, qaug_ref, qa, ka, va):
    total = qa.shape[0]
    keys = ka.shape[1]
    head = q_ref.shape[1] // 2
    qa[0:rows, 0:LANES] = q_ref[...] * jnp.asarray(scale, bf16)
    qa[0:rows, LANES:] = qmark_ref[...]
    lane_k = lane_index(rows)
    for j in range(2):
        own = (lane_k >= head * j) & (lane_k < head * (j + 1))
        k_own = jnp.where(own, k_ref[...], jnp.zeros_like(k_ref))
        ka[j, 0:rows, 0:LANES] = k_own
        ka[j, 0:rows, LANES:] = kmark_ref[...]
        ones = jnp.where(lane_k == head * (1 - j), jnp.ones_like(v_ref), jnp.zeros_like(v_ref))
        va[j, 0:rows, :] = jnp.where(own, v_ref[...], ones)
        va[j, rows:, :] = jnp.zeros((keys - rows, LANES), bf16)
        ka[j, rows:, 0:LANES] = jnp.zeros((keys - rows, LANES), bf16)
        lane_pad = lane_index(keys - rows)
        ka[j, rows:, LANES:] = jnp.where(lane_pad < 3, masked_score, 0.0).astype(bf16)
    if total > rows:
        lane_pad = lane_index(total - rows)
        qa[rows:, 0:LANES] = jnp.zeros((total - rows, LANES), bf16)
        qa[rows:, LANES:] = jnp.where(lane_pad == 0, 1.0, 0.0).astype(bf16)
    lane = lane_index(chunk)
    for start in range(0, total, chunk):
        q_rows = qa[start : start + chunk, :]
        outs = []
        size = min(chunk, rows - start)
        for j in range(2):
            scores = dot_nt(q_rows, ka[j])
            row_max = jnp.max(scores, axis=1, keepdims=True)
            probs = jnp.exp(scores - row_max).astype(bf16)
            out = dot_nn(probs, va[j])
            row_sum = out[:, head * (1 - j) : head * (1 - j) + 1]
            outs.append(out / row_sum)
            log_total = row_max + jnp.log(row_sum)
            aug = split_three(-log_total, lane, q_rows[:, LANES:].astype(f32))
            qaug_ref[start : start + size, j * LANES : (j + 1) * LANES] = aug[:size]
        both = jnp.where(lane < head, outs[0], outs[1]).astype(bf16)
        out_ref[start : start + size, :] = both[:size]


def attention_forward(packed, qmark, kmark, chunk=304):
    rows, width = packed.shape[0], packed.shape[1] // 3
    pairs = width // LANES
    total, keys = padded(rows, 16), padded(rows, 256)
    if total % chunk:
        chunk = total
    kernel = functools.partial(attention_forward_kernel, (width // H) ** (-0.5), rows, chunk)
    block = lambda offset: pl.BlockSpec((rows, LANES), lambda g: (0, g + offset))
    fixed = pl.BlockSpec((rows, LANES), lambda g: (0, 0))
    return pl.pallas_call(
        kernel,
        grid=(pairs,),
        in_specs=[block(0), block(pairs), block(2 * pairs), fixed, fixed],
        out_specs=[pl.BlockSpec((rows, LANES), lambda g: (0, g)), pl.BlockSpec((rows, 2 * LANES), lambda g: (0, g))],
        out_shape=[
            jax.ShapeDtypeStruct((rows, width), bf16),
            jax.ShapeDtypeStruct((rows, 2 * width), bf16),
        ],
        scratch_shapes=[
            pltpu.VMEM((total, 2 * LANES), bf16),
            pltpu.VMEM((2, keys, 2 * LANES), bf16),
            pltpu.VMEM((2, keys, LANES), bf16),
        ],
        name="attention_forward",
    )(packed, packed, packed, qmark, kmark)


def attention_backward_kernel(scale, rows, chunk, first, q_ref, k_ref, v_ref, go_ref, out_ref, qaug_ref, kmark_ref, *rest):
    grad_ref, qa, da, ka, va, kt, dqt, found, sems = rest[-9:]
    step = pl.program_id(0)
    dq_ref, dk_ref, dv_ref = found.at[step, 0], found.at[step, 1], found.at[step, 2]
    queries = qa.shape[1]
    total = ka.shape[0]
    head = q_ref.shape[1] // 2
    lane = lane_index(rows)
    ka[0:rows, 0:LANES] = k_ref[...]
    ka[0:rows, LANES:] = kmark_ref[...]
    va[0:rows, 0:LANES] = v_ref[...]
    ones = jnp.where((lane >= 3) & (lane < 6), 1.0, 0.0).astype(bf16)
    va[0:rows, LANES:] = ones
    if total > rows:
        pad = total - rows
        ka[rows:, 0:LANES] = jnp.zeros((pad, LANES), bf16)
        ka[rows:, LANES:] = jnp.where(lane_index(pad) < 3, masked_score, 0.0).astype(bf16)
        va[rows:, :] = jnp.zeros((pad, 2 * LANES), bf16)
    kt[...] = ka[:, 0:LANES].astype(f32).T.astype(bf16)
    for j in range(2):
        own = (lane >= head * j) & (lane < head * (j + 1))
        qa[j, 0:rows, 0:LANES] = jnp.where(own, q_ref[...] * jnp.asarray(scale, bf16), jnp.zeros_like(q_ref))
        qa[j, 0:rows, LANES:] = qaug_ref[:, j * LANES : (j + 1) * LANES]
        go = jnp.where(own, go_ref[...], jnp.zeros_like(go_ref))
        delta = jnp.sum(go.astype(f32) * out_ref[...].astype(f32), axis=1, keepdims=True)
        da[j, 0:rows, 0:LANES] = go
        da[j, 0:rows, LANES:] = split_three(-delta, lane, 0.0)
        qa[j, rows:, :] = jnp.zeros((queries - rows, 2 * LANES), bf16)
        da[j, rows:, :] = jnp.zeros((queries - rows, 2 * LANES), bf16)
    for start in range(0, total, chunk):
        here = slice(start, start + chunk)
        dk = dv = None
        size = min(chunk, rows - start)
        for j in range(2):
            probs = jnp.exp(dot_nt(ka[here, :], qa[j]))
            grad_probs = dot_nt(va[here, :], da[j])
            grad_scores = (probs * grad_probs).astype(bf16)
            dv_part = dot_nn(probs.astype(bf16), da[j, :, 0:LANES])
            dk_part = dot_nn(grad_scores, qa[j, :, 0:LANES])
            dq_part = dot_nn(kt[j * head : (j + 1) * head, here], grad_scores)
            spot = slice(j * head, (j + 1) * head)
            dqt[spot, :] = dq_part if start == 0 else dqt[spot, :] + dq_part
            dk = dk_part if dk is None else dk + dk_part
            dv = dv_part if dv is None else dv + dv_part
        dk_ref[start : start + size, :] = dk.astype(bf16)[:size]
        dv_ref[start : start + size, :] = dv.astype(bf16)[:size]
    dq_ref[...] = (dqt[...].T * scale).astype(bf16)[:rows]

    def copy_of(at, which):
        column = LANES * first + LANES * at + which * (grad_ref.shape[1] // 3)
        spot = pl.ds(pl.multiple_of(column, LANES), LANES)
        return pltpu.make_async_copy(
            found.at[at, which], grad_ref.at[:, spot], sems.at[at, which]
        )

    for which in range(3):
        copy_of(step, which).start()

    @pl.when(step == pl.num_programs(0) - 1)
    def _():
        for at in range(found.shape[0]):
            for which in range(3):
                copy_of(at, which).wait()


def attention_backward(packed, grad_attended, attended, qaug, kmark, first, count, before=None, chunk=912):
    rows, width = packed.shape[0], packed.shape[1] // 3
    pairs = width // LANES
    queries = padded(rows, 256)
    total = padded(rows, 16)
    if total % chunk:
        chunk = total
    kernel = functools.partial(attention_backward_kernel, (width // H) ** (-0.5), rows, chunk, first)
    block = lambda offset: pl.BlockSpec((rows, LANES), lambda g: (0, g + offset + first))
    anywhere = pl.BlockSpec(memory_space=pl.ANY)
    fixed = pl.BlockSpec((rows, LANES), lambda g: (0, 0))
    return pl.pallas_call(
        kernel,
        grid=(count,),
        in_specs=[block(0), block(pairs), block(2 * pairs), block(0), block(0), pl.BlockSpec((rows, 2 * LANES), lambda g: (0, g + first)), fixed] + ([] if before is None else [anywhere]),
        out_specs=anywhere,
        out_shape=jax.ShapeDtypeStruct((rows, 3 * width), bf16),
        scratch_shapes=[
            pltpu.VMEM((2, queries, 2 * LANES), bf16),
            pltpu.VMEM((2, queries, 2 * LANES), bf16),
            pltpu.VMEM((total, 2 * LANES), bf16),
            pltpu.VMEM((total, 2 * LANES), bf16),
            pltpu.VMEM((LANES, total), bf16),
            pltpu.VMEM((LANES, queries), f32),
            pltpu.VMEM((count, 3, rows, LANES), bf16),
            pltpu.SemaphoreType.DMA((count, 3)),
        ],
        input_output_aliases={} if before is None else {7: 0},
        name="attention_backward",
    )(packed, packed, packed, grad_attended, attended, qaug, kmark, *([] if before is None else [before]))


def marks(row_item, row_live):
    rows = row_item.shape[0]
    lane = lane_index(rows)
    item = row_item[:, None] == lane
    qmark = item.astype(bf16)
    barred = (lane < 3) & ~(item & (row_live[:, None] == 1))
    kmark = jnp.where(barred, masked_score, jnp.where((lane >= 3) & (lane < 6), 1.0, 0.0)).astype(bf16)
    return qmark, kmark


def place_kernel(half, place_ref, own, near, far, own_c, near_c, far_c, out_ref, sems):
    f, low = place_ref[0], place_ref[1]
    copies = []
    for at, (base, piece_own, piece_near, piece_far) in enumerate(
        ((f, own, near, far), (f ^ 1, own_c, near_c, far_c))
    ):
        begin = 2 * half * (base ^ 2)
        spots = (
            (piece_own, 2 * half * base, 2 * half),
            (piece_near, begin + half * low, half),
            (piece_far, begin + half * (1 - low), half),
        )
        for spot, (piece, start, size) in enumerate(spots):
            rows = pl.ds(pl.multiple_of(start, half), size)
            copies.append(
                pltpu.make_async_copy(piece, out_ref.at[rows, :], sems.at[3 * at + spot])
            )
    for copy in copies:
        copy.start()
    for copy in copies:
        copy.wait()


def gather_rows(shard, name, *gates):
    rows, columns = shard.shape
    half = rows // 2
    n_group, n_data = lax.axis_size("fsdp"), lax.axis_size("dp")
    low = lax.axis_index("dp") & 1
    if gates:
        shard = after(shard, *gates)
    send = lax.dynamic_slice_in_dim(shard, half * low, half, 0)
    with jax.named_scope(name + "_near"):
        near = lax.ppermute(send, "fsdp", bit_pairs(n_group, 1))
    with jax.named_scope(name + "_own_c"):
        own_c = lax.ppermute(shard, "fsdp", bit_pairs(n_group, 0))
    with jax.named_scope(name + "_far"):
        far = lax.ppermute(near, "dp", bit_pairs(n_data, 0))
    with jax.named_scope(name + "_near_c"):
        near_c = lax.ppermute(near, "fsdp", bit_pairs(n_group, 0))
    with jax.named_scope(name + "_far_c"):
        far_c = lax.ppermute(far, "fsdp", bit_pairs(n_group, 0))
    place = jnp.stack([lax.axis_index("fsdp"), low]).astype(jnp.int32)
    anywhere = pl.BlockSpec(memory_space=pl.ANY)
    full = pl.pallas_call(
        functools.partial(place_kernel, half),
        in_specs=[pl.BlockSpec(memory_space=pltpu.SMEM)] + [anywhere] * 6,
        out_specs=pl.BlockSpec(memory_space=pltpu.VMEM),
        out_shape=jax.ShapeDtypeStruct((n_group * rows, columns), shard.dtype),
        scratch_shapes=[pltpu.SemaphoreType.DMA((6,))],
        name=name,
    )(place, shard, near, far, own_c, near_c, far_c)
    return full, near


def gather_vectors(members, *gates):
    n_group = lax.axis_size("fsdp")
    f = lax.axis_index("fsdp")
    size = members[0].shape[0]
    rows = [row for member in members for row in member.reshape(-1, size)]
    spot = lax.broadcasted_iota(jnp.int32, (padded(len(rows), 16), size), 0)
    packed = jnp.zeros(spot.shape, bf16)
    for at, row in enumerate(rows):
        packed = jnp.where(spot == at, row[None, :], packed)
    packed = after(packed, *gates)[None]
    pair = lax.ppermute(packed, "fsdp", bit_pairs(n_group, 1))
    both = jnp.concatenate([packed, pair], 0)
    core = lax.ppermute(both, "fsdp", bit_pairs(n_group, 0))
    found = [both[0], core[0], both[1], core[1]]
    ordered = jnp.stack(
        [
            sum(
                jnp.where((f ^ at) == away, found[away], jnp.zeros_like(found[away]))
                for away in range(n_group)
            )
            for at in range(n_group)
        ]
    ).astype(f32)
    outs, start = [], 0
    for member in members:
        count = member.shape[0] // size
        outs.append(ordered[:, start : start + count].reshape(-1))
        start += count
    return outs


def shards(
    inputs,
    skip_input,
    cotangent,
    row_item,
    row_live,
    skip_weight,
    skip_bias,
    attn_gain,
    attn_shift,
    qkv_weight,
    proj_weight,
    proj_bias,
    mlp_gain,
    mlp_shift,
    hidden_weight,
    hidden_bias,
    output_weight,
    output_bias,
):
    model_width = inputs.shape[1]
    skip_full, skip_near = gather_rows(skip_weight, "place_skip")
    (
        skip_vec,
        gain_first,
        shift_first,
        proj_vec,
        gain_second,
        shift_second,
        hidden_vec,
        output_vec,
    ) = gather_vectors(
        [
            skip_bias,
            attn_gain,
            attn_shift,
            proj_bias,
            mlp_gain,
            mlp_shift,
            hidden_bias,
            output_bias,
        ],
    )
    qkv_full, qkv_near = gather_rows(qkv_weight, "place_qkv", skip_near)
    proj_full, _ = gather_rows(proj_weight, "place_proj", qkv_near)
    hidden_full, _ = gather_rows(hidden_weight, "place_hidden", qkv_near)
    output_full, _ = gather_rows(output_weight, "place_output", qkv_near)
    joined = jnp.concatenate([inputs, skip_input], axis=1)
    stream_a = times_t(joined, skip_full) + skip_vec
    normed_a = layer_norm(stream_a, gain_first, shift_first).astype(jnp.bfloat16)
    packed = times_t(normed_a, qkv_full).astype(jnp.bfloat16)
    qmark, kmark = marks(row_item, row_live)
    attended, qaug = attention_forward(packed, qmark, kmark)
    stream_b = stream_a + times_t(attended, proj_full) + proj_vec
    normed_b = layer_norm(stream_b, gain_second, shift_second).astype(jnp.bfloat16)
    pre_act = times_t(normed_b, hidden_full) + hidden_vec
    activation = jax.nn.gelu(pre_act, approximate=False).astype(jnp.bfloat16)
    grad_out = cotangent * row_live[:, None].astype(jnp.bfloat16)
    grad_output_weight = rows_outer(grad_out, activation).astype(bf16)
    reduce_out = Reducer("out", grad_output_weight)
    sent = reduce_out.step()
    grad_act = times_n(after(grad_out, sent), output_full)
    gelu_value, gelu_back = jax.vjp(lambda value: jax.nn.gelu(value, approximate=False), pre_act)
    grad_pre = gelu_back(grad_act)[0].astype(jnp.bfloat16)
    sent = reduce_out.step(grad_pre)
    grad_hidden_weight = rows_outer(after(grad_pre, sent), normed_b).astype(bf16)
    grad_hidden_bias = column_sums(grad_pre)
    grad_normed_b = times_n(after(grad_pre, grad_hidden_weight), hidden_full)
    norm_value, norm_back = jax.vjp(layer_norm, stream_b, gain_second, shift_second)
    grad_part_b, grad_mlp_gain, grad_mlp_shift = norm_back(grad_normed_b)
    grad_stream_b = grad_out.astype(jnp.float32) + grad_part_b
    grad_branch = grad_stream_b.astype(jnp.bfloat16)
    grad_proj_weight = rows_outer(grad_branch, attended).astype(bf16)
    grad_proj_bias = column_sums(grad_branch)
    grad_attended = times_n(grad_branch, proj_full).astype(jnp.bfloat16)
    reduce_mlp = Reducer("mlp", grad_hidden_weight, grad_proj_weight)
    sent = [reduce_mlp.step(), reduce_out.step(grad_attended)]
    pairs = model_width // LANES
    cuts = [pairs * third // 3 for third in range(4)]
    grad_qkv = None
    for third in range(3):
        with jax.named_scope(f"bwd_a{third}"):
            grad_qkv = attention_backward(
                packed, after(grad_attended, *sent), attended, qaug, kmark,
                cuts[third], cuts[third + 1] - cuts[third], grad_qkv,
            )
        sent = [reduce_out.step(grad_qkv)]
        if third != 1:
            sent.append(reduce_mlp.step(grad_qkv))
    grad_qkv_weight = rows_outer(after(grad_qkv, sent), normed_a).astype(bf16)
    reduce_qkv = Reducer("qkv", grad_qkv_weight)
    sent = [
        reduce_qkv.step(),
        reduce_out.step(grad_qkv_weight),
    ]
    grad_normed_a = times_n(after(grad_qkv, *sent), qkv_full)
    sent = [
        reduce_qkv.step(grad_normed_a),
        reduce_mlp.step(grad_normed_a),
    ]
    first_value, first_back = jax.vjp(layer_norm, stream_a, gain_first, shift_first)
    grad_part_a, grad_attn_gain, grad_attn_shift = first_back(after(grad_normed_a, *sent))
    grad_rounded = (grad_stream_b + grad_part_a).astype(jnp.bfloat16)
    sent = reduce_mlp.step(grad_rounded)
    grad_skip_weight = rows_outer(after(grad_rounded, sent), joined)
    grad_skip_bias = column_sums(grad_rounded)
    grad_output_bias = column_sums(grad_out)
    n_group = lax.axis_size("fsdp")
    rows = model_width // n_group
    vectors = jnp.stack(
        [
            grad_skip_bias,
            grad_attn_gain,
            grad_attn_shift,
            grad_proj_bias,
            grad_mlp_gain,
            grad_mlp_shift,
            grad_output_bias,
        ]
    )
    wide = grad_hidden_bias.reshape(n_group, -1, rows)
    wide_count = wide.shape[1]
    wide = jnp.swapaxes(wide, 0, 1).reshape(wide_count, model_width)
    vectors = jnp.concatenate([vectors, wide], 0)
    vectors = jnp.pad(vectors, ((0, LANES - vectors.shape[0]), (0, 0))).T
    last = jnp.concatenate([grad_skip_weight, vectors], 1).astype(jnp.bfloat16)
    reduce_last = Reducer("last", last)
    sent = [reduce_last.step(), reduce_mlp.step(last)]
    grad_joined = times_n(after(grad_rounded, *sent), skip_full)
    grad_input = grad_joined[:, :model_width].astype(jnp.bfloat16)
    grad_skip = grad_joined[:, model_width:].astype(jnp.bfloat16)
    sent = [
        reduce_last.step(grad_input, grad_skip),
        reduce_mlp.step(grad_input),
        reduce_qkv.step(grad_input),
    ]
    output = (
        stream_b + times_t(after(activation, *sent), output_full) + output_vec
    ).astype(jnp.bfloat16)
    gate = output
    for turn in range(len(reduce_last.plan)):
        gate = after(reduce_qkv.step(gate), reduce_last.step(gate))
    final_output = reduce_out.finish(output)
    both_final = reduce_mlp.finish(output)
    final_hidden = both_final[: hidden_weight.shape[0]]
    final_proj = both_final[hidden_weight.shape[0] :]
    final_qkv = reduce_qkv.finish()
    last = reduce_last.finish()
    final_skip = last[:, : 2 * model_width]
    final_vec = last[:, 2 * model_width :].T
    final_wide = final_vec[7 : 7 + wide_count].reshape(-1)
    return (
        output,
        grad_input,
        grad_skip,
        final_skip,
        final_vec[0],
        final_vec[1],
        final_vec[2],
        final_qkv,
        final_proj,
        final_vec[3],
        final_vec[4],
        final_vec[5],
        final_hidden,
        final_wide,
        final_output,
        final_vec[6],
    )


def solution(mesh):
    in_specs = (
        P(("dp", "fsdp"), None),
        P(("dp", "fsdp"), None),
        P(("dp", "fsdp"), None),
        P(("dp", "fsdp")),
        P(("dp", "fsdp")),
        P("fsdp", None),
        P("fsdp"),
        P("fsdp"),
        P("fsdp"),
        P("fsdp", None),
        P("fsdp", None),
        P("fsdp"),
        P("fsdp"),
        P("fsdp"),
        P("fsdp", None),
        P("fsdp"),
        P("fsdp", None),
        P("fsdp"),
    )
    out_specs = (
        P(("dp", "fsdp"), None),
        P(("dp", "fsdp"), None),
        P(("dp", "fsdp"), None),
        P("fsdp", None),
        P("fsdp"),
        P("fsdp"),
        P("fsdp"),
        P("fsdp", None),
        P("fsdp", None),
        P("fsdp"),
        P("fsdp"),
        P("fsdp"),
        P("fsdp", None),
        P("fsdp"),
        P("fsdp", None),
        P("fsdp"),
    )
    return jax.shard_map(shards, mesh=mesh, in_specs=in_specs, out_specs=out_specs, check_vma=False)
```

```python
import functools

import jax
import jax.numpy as jnp
from jax import lax
from jax.experimental import pallas as pl
from jax.experimental.pallas import tpu as pltpu
from jax.sharding import PartitionSpec as P

H = 12


epsilon = 1e-05
masked_score = -1e30


def layer_norm(stream, norm_gain, norm_shift):
    row_mean = jnp.mean(stream, axis=1, keepdims=True)
    centred = stream - row_mean
    row_var = jnp.mean(centred * centred, axis=1, keepdims=True)
    return centred * lax.rsqrt(row_var + epsilon) * norm_gain + norm_shift


def times_t(left, weight):
    return lax.dot_general(
        left, weight, (((1,), (1,)), ((), ())), preferred_element_type=jnp.float32
    )


def times_n(left, weight):
    return jnp.dot(left, weight, preferred_element_type=jnp.float32)


def rows_outer(grad_rows, left):
    return lax.dot_general(
        grad_rows, left, (((0,), (0,)), ((), ())), preferred_element_type=jnp.float32
    )


def column_sums(grad_rows):
    return jnp.sum(grad_rows.astype(jnp.float32), axis=0)


def bit_pairs(count, bit):
    return [(place, place ^ (1 << bit)) for place in range(count)]


def add_low(first, second):
    return (first.astype(jnp.float32) + second.astype(jnp.float32)).astype(jnp.bfloat16)


def after(value, *gates):
    return lax.optimization_barrier((value,) + gates)[0]


class Reducer:
    def __init__(self, *grads):
        self.n_group, self.n_data = lax.axis_size("fsdp"), lax.axis_size("dp")
        columns = grads[0].shape[1]
        self.parts = [grad.reshape(self.n_group, -1, columns) for grad in grads]
        bits = self.n_data.bit_length() - 1
        self.plan = [("fsdp", bit, "halve") for bit in range(self.n_group.bit_length() - 1)]
        self.plan += [("dp", bit, "halve") for bit in range(bits - 1)]
        self.plan += [("dp", bits - 1, "swap")]
        self.plan += [("dp", bit, "join") for bit in reversed(range(bits - 1))]
        self.flight = None
        self.at = 0

    def take(self, gates):
        if self.flight is None:
            return
        got = after(self.flight, *gates)
        axis, bit, kind = self.plan[self.at - 1]
        if kind == "join":
            low = ((lax.axis_index(axis) >> bit) & 1) == 0
            part = self.parts[0]
            part = jnp.where(
                low, jnp.concatenate([part, got], 1), jnp.concatenate([got, part], 1)
            )
        else:
            part = add_low(self.keep, got)
        self.parts = [part]

    def step(self, *gates):
        if self.at == len(self.plan):
            return self.parts[0]
        self.take(gates)
        axis, bit, kind = self.plan[self.at]
        self.at += 1
        if kind == "halve":
            mine = (lax.axis_index(axis) >> bit) & 1
            keeps, sends = [], []
            for part in self.parts:
                columns = part.shape[-1]
                if axis == "fsdp":
                    stack = part.reshape(part.shape[0] // 2, 2, -1, columns)
                else:
                    stack = part.reshape(1, 2, -1, columns)
                keeps.append(lax.dynamic_index_in_dim(stack, mine, 1, keepdims=False))
                sends.append(lax.dynamic_index_in_dim(stack, 1 - mine, 1, keepdims=False))
            self.keep = keeps[0] if len(keeps) == 1 else jnp.concatenate(keeps, 1)
            send = sends[0] if len(sends) == 1 else jnp.concatenate(sends, 1)
        else:
            send = self.keep = self.parts[0]
        self.flight = lax.ppermute(send, axis, bit_pairs(lax.axis_size(axis), bit))
        return send

    def finish(self, *gates):
        while self.at < len(self.plan):
            self.step(*gates)
        self.take(gates)
        return self.parts[0][0].astype(jnp.float32) / (self.n_group * self.n_data)


LANES = 128
f32, bf16 = jnp.float32, jnp.bfloat16
NT = (((1,), (1,)), ((), ()))
NN = (((1,), (0,)), ((), ()))


def dot_nt(left, right):
    return lax.dot_general(left, right, NT, preferred_element_type=f32)


def dot_nn(left, right):
    return lax.dot_general(left, right, NN, preferred_element_type=f32)


def lane_index(rows):
    return lax.broadcasted_iota(jnp.int32, (rows, LANES), 1)


def split_three(column, lane, rest):
    high = column.astype(bf16).astype(f32)
    middle = (column - high).astype(bf16).astype(f32)
    low = column - high - middle
    wide = jnp.where(lane == 3, high, jnp.where(lane == 4, middle, jnp.where(lane == 5, low, rest)))
    return wide.astype(bf16)


def padded(count, step):
    return -(-count // step) * step


def attention_forward_kernel(scale, rows, chunk, q_ref, k_ref, v_ref, qmark_ref, kmark_ref, out_ref, qaug_ref, qa, ka, va):
    total = qa.shape[0]
    keys = ka.shape[1]
    head = q_ref.shape[1] // 2
    qa[0:rows, 0:LANES] = q_ref[...] * jnp.asarray(scale, bf16)
    qa[0:rows, LANES:] = qmark_ref[...]
    lane_k = lane_index(rows)
    for j in range(2):
        own = (lane_k >= head * j) & (lane_k < head * (j + 1))
        k_own = jnp.where(own, k_ref[...], jnp.zeros_like(k_ref))
        ka[j, 0:rows, 0:LANES] = k_own
        ka[j, 0:rows, LANES:] = kmark_ref[...]
        ones = jnp.where(lane_k == head * (1 - j), jnp.ones_like(v_ref), jnp.zeros_like(v_ref))
        va[j, 0:rows, :] = jnp.where(own, v_ref[...], ones)
        va[j, rows:, :] = jnp.zeros((keys - rows, LANES), bf16)
        ka[j, rows:, 0:LANES] = jnp.zeros((keys - rows, LANES), bf16)
        lane_pad = lane_index(keys - rows)
        ka[j, rows:, LANES:] = jnp.where(lane_pad < 3, masked_score, 0.0).astype(bf16)
    if total > rows:
        lane_pad = lane_index(total - rows)
        qa[rows:, 0:LANES] = jnp.zeros((total - rows, LANES), bf16)
        qa[rows:, LANES:] = jnp.where(lane_pad == 0, 1.0, 0.0).astype(bf16)
    lane = lane_index(chunk)
    for start in range(0, total, chunk):
        q_rows = qa[start : start + chunk, :]
        outs = []
        size = min(chunk, rows - start)
        for j in range(2):
            scores = dot_nt(q_rows, ka[j])
            row_max = jnp.max(scores, axis=1, keepdims=True)
            probs = jnp.exp(scores - row_max).astype(bf16)
            out = dot_nn(probs, va[j])
            row_sum = out[:, head * (1 - j) : head * (1 - j) + 1]
            outs.append(out / row_sum)
            log_total = row_max + jnp.log(row_sum)
            aug = split_three(-log_total, lane, q_rows[:, LANES:].astype(f32))
            qaug_ref[start : start + size, j * LANES : (j + 1) * LANES] = aug[:size]
        both = jnp.where(lane < head, outs[0], outs[1]).astype(bf16)
        out_ref[start : start + size, :] = both[:size]


def attention_forward(packed, qmark, kmark, chunk=304):
    rows, width = packed.shape[0], packed.shape[1] // 3
    pairs = width // LANES
    total, keys = padded(rows, 16), padded(rows, 256)
    if total % chunk:
        chunk = total
    kernel = functools.partial(attention_forward_kernel, (width // H) ** (-0.5), rows, chunk)
    block = lambda offset: pl.BlockSpec((rows, LANES), lambda g: (0, g + offset))
    fixed = pl.BlockSpec((rows, LANES), lambda g: (0, 0))
    return pl.pallas_call(
        kernel,
        grid=(pairs,),
        in_specs=[block(0), block(pairs), block(2 * pairs), fixed, fixed],
        out_specs=[pl.BlockSpec((rows, LANES), lambda g: (0, g)), pl.BlockSpec((rows, 2 * LANES), lambda g: (0, g))],
        out_shape=[
            jax.ShapeDtypeStruct((rows, width), bf16),
            jax.ShapeDtypeStruct((rows, 2 * width), bf16),
        ],
        scratch_shapes=[
            pltpu.VMEM((total, 2 * LANES), bf16),
            pltpu.VMEM((2, keys, 2 * LANES), bf16),
            pltpu.VMEM((2, keys, LANES), bf16),
        ],
        name="attention_forward",
    )(packed, packed, packed, qmark, kmark)


def attention_backward_kernel(scale, rows, chunk, first, q_ref, k_ref, v_ref, go_ref, out_ref, qaug_ref, kmark_ref, *rest):
    grad_ref, qa, da, ka, va, kt, dqt, found, sems = rest[-9:]
    step = pl.program_id(0)
    dq_ref, dk_ref, dv_ref = found.at[step, 0], found.at[step, 1], found.at[step, 2]
    queries = qa.shape[1]
    total = ka.shape[0]
    head = q_ref.shape[1] // 2
    lane = lane_index(rows)
    ka[0:rows, 0:LANES] = k_ref[...]
    ka[0:rows, LANES:] = kmark_ref[...]
    va[0:rows, 0:LANES] = v_ref[...]
    ones = jnp.where((lane >= 3) & (lane < 6), 1.0, 0.0).astype(bf16)
    va[0:rows, LANES:] = ones
    if total > rows:
        pad = total - rows
        ka[rows:, 0:LANES] = jnp.zeros((pad, LANES), bf16)
        ka[rows:, LANES:] = jnp.where(lane_index(pad) < 3, masked_score, 0.0).astype(bf16)
        va[rows:, :] = jnp.zeros((pad, 2 * LANES), bf16)
    kt[...] = ka[:, 0:LANES].astype(f32).T.astype(bf16)
    for j in range(2):
        own = (lane >= head * j) & (lane < head * (j + 1))
        qa[j, 0:rows, 0:LANES] = jnp.where(own, q_ref[...] * jnp.asarray(scale, bf16), jnp.zeros_like(q_ref))
        qa[j, 0:rows, LANES:] = qaug_ref[:, j * LANES : (j + 1) * LANES]
        go = jnp.where(own, go_ref[...], jnp.zeros_like(go_ref))
        delta = jnp.sum(go.astype(f32) * out_ref[...].astype(f32), axis=1, keepdims=True)
        da[j, 0:rows, 0:LANES] = go
        da[j, 0:rows, LANES:] = split_three(-delta, lane, 0.0)
        qa[j, rows:, :] = jnp.zeros((queries - rows, 2 * LANES), bf16)
        da[j, rows:, :] = jnp.zeros((queries - rows, 2 * LANES), bf16)
    for start in range(0, total, chunk):
        here = slice(start, start + chunk)
        dk = dv = None
        size = min(chunk, rows - start)
        for j in range(2):
            probs = jnp.exp(dot_nt(ka[here, :], qa[j]))
            grad_probs = dot_nt(va[here, :], da[j])
            grad_scores = (probs * grad_probs).astype(bf16)
            dv_part = dot_nn(probs.astype(bf16), da[j, :, 0:LANES])
            dk_part = dot_nn(grad_scores, qa[j, :, 0:LANES])
            dq_part = dot_nn(kt[j * head : (j + 1) * head, here], grad_scores)
            spot = slice(j * head, (j + 1) * head)
            dqt[spot, :] = dq_part if start == 0 else dqt[spot, :] + dq_part
            dk = dk_part if dk is None else dk + dk_part
            dv = dv_part if dv is None else dv + dv_part
        dk_ref[start : start + size, :] = dk.astype(bf16)[:size]
        dv_ref[start : start + size, :] = dv.astype(bf16)[:size]
    dq_ref[...] = (dqt[...].T * scale).astype(bf16)[:rows]

    def copy_of(at, which):
        column = LANES * first + LANES * at + which * (grad_ref.shape[1] // 3)
        spot = pl.ds(pl.multiple_of(column, LANES), LANES)
        return pltpu.make_async_copy(
            found.at[at, which], grad_ref.at[:, spot], sems.at[at, which]
        )

    for which in range(3):
        copy_of(step, which).start()

    @pl.when(step == pl.num_programs(0) - 1)
    def _():
        for at in range(found.shape[0]):
            for which in range(3):
                copy_of(at, which).wait()


def attention_backward(packed, grad_attended, attended, qaug, kmark, first, count, before=None, chunk=912):
    rows, width = packed.shape[0], packed.shape[1] // 3
    pairs = width // LANES
    queries = padded(rows, 256)
    total = padded(rows, 16)
    if total % chunk:
        chunk = total
    kernel = functools.partial(attention_backward_kernel, (width // H) ** (-0.5), rows, chunk, first)
    block = lambda offset: pl.BlockSpec((rows, LANES), lambda g: (0, g + offset + first))
    anywhere = pl.BlockSpec(memory_space=pl.ANY)
    fixed = pl.BlockSpec((rows, LANES), lambda g: (0, 0))
    return pl.pallas_call(
        kernel,
        grid=(count,),
        in_specs=[block(0), block(pairs), block(2 * pairs), block(0), block(0), pl.BlockSpec((rows, 2 * LANES), lambda g: (0, g + first)), fixed] + ([] if before is None else [anywhere]),
        out_specs=anywhere,
        out_shape=jax.ShapeDtypeStruct((rows, 3 * width), bf16),
        scratch_shapes=[
            pltpu.VMEM((2, queries, 2 * LANES), bf16),
            pltpu.VMEM((2, queries, 2 * LANES), bf16),
            pltpu.VMEM((total, 2 * LANES), bf16),
            pltpu.VMEM((total, 2 * LANES), bf16),
            pltpu.VMEM((LANES, total), bf16),
            pltpu.VMEM((LANES, queries), f32),
            pltpu.VMEM((count, 3, rows, LANES), bf16),
            pltpu.SemaphoreType.DMA((count, 3)),
        ],
        input_output_aliases={} if before is None else {7: 0},
        name="attention_backward",
    )(packed, packed, packed, grad_attended, attended, qaug, kmark, *([] if before is None else [before]))


def hidden_kernel(normed_ref, weight_ref, bias_ref, act_ref, slope_ref):
    pre_act = dot_nt(normed_ref[...], weight_ref[...]) + bias_ref[...]
    t = 1.0 / (1.0 + 0.23164189 * jnp.abs(pre_act))
    bell = jnp.exp(-0.5 * pre_act * pre_act)
    tail = 0.5307027145 * t - 0.7265760135
    tail = (tail * t + 0.7107068705) * t - 0.142248368
    tail = (tail * t + 0.127414796) * t * bell
    normal = jnp.where(pre_act >= 0, 1.0 - tail, tail)
    act_ref[...] = (pre_act * normal).astype(bf16)
    slope_ref[...] = (normal + 0.3989422804 * pre_act * bell).astype(bf16)


def hidden_forward(normed, weight, bias, step=256):
    rows, width = normed.shape
    hidden = weight.shape[0]
    block = pl.BlockSpec((rows, step), lambda g: (0, g))
    return pl.pallas_call(
        hidden_kernel,
        grid=(hidden // step,),
        in_specs=[
            pl.BlockSpec((rows, width), lambda g: (0, 0)),
            pl.BlockSpec((step, width), lambda g: (g, 0)),
            pl.BlockSpec((1, step), lambda g: (0, g)),
        ],
        out_specs=[block, block],
        out_shape=[jax.ShapeDtypeStruct((rows, hidden), bf16)] * 2,
        name="hidden_forward",
    )(normed, weight, bias[None, :])


def marks(row_item, row_live):
    rows = row_item.shape[0]
    lane = lane_index(rows)
    item = row_item[:, None] == lane
    qmark = item.astype(bf16)
    barred = (lane < 3) & ~(item & (row_live[:, None] == 1))
    kmark = jnp.where(barred, masked_score, jnp.where((lane >= 3) & (lane < 6), 1.0, 0.0)).astype(bf16)
    return qmark, kmark


def place_kernel(half, place_ref, own, near, far, own_c, near_c, far_c, out_ref, sems):
    f, low = place_ref[0], place_ref[1]
    copies = []
    for at, (base, piece_own, piece_near, piece_far) in enumerate(
        ((f, own, near, far), (f ^ 1, own_c, near_c, far_c))
    ):
        begin = 2 * half * (base ^ 2)
        spots = (
            (piece_own, 2 * half * base, 2 * half),
            (piece_near, begin + half * low, half),
            (piece_far, begin + half * (1 - low), half),
        )
        for spot, (piece, start, size) in enumerate(spots):
            rows = pl.ds(pl.multiple_of(start, half), size)
            copies.append(
                pltpu.make_async_copy(piece, out_ref.at[rows, :], sems.at[3 * at + spot])
            )
    for copy in copies:
        copy.start()
    for copy in copies:
        copy.wait()


def gather_start(shard, *gates):
    rows, _ = shard.shape
    half = rows // 2
    n_group = lax.axis_size("fsdp")
    low = lax.axis_index("dp") & 1
    if gates:
        shard = after(shard, *gates)
    send = lax.dynamic_slice_in_dim(shard, half * low, half, 0)
    near = lax.ppermute(send, "fsdp", bit_pairs(n_group, 1))
    own_c = lax.ppermute(shard, "fsdp", bit_pairs(n_group, 0))
    return shard, near, own_c


def gather_finish(started, *gates):
    shard, near, own_c = started
    half, columns = shard.shape[0] // 2, shard.shape[1]
    rows = 2 * half
    n_group, n_data = lax.axis_size("fsdp"), lax.axis_size("dp")
    low = lax.axis_index("dp") & 1
    if gates:
        near = after(near, *gates)
    far = lax.ppermute(near, "dp", bit_pairs(n_data, 0))
    near_c = lax.ppermute(near, "fsdp", bit_pairs(n_group, 0))
    far_c = lax.ppermute(far, "fsdp", bit_pairs(n_group, 0))
    place = jnp.stack([lax.axis_index("fsdp"), low]).astype(jnp.int32)
    anywhere = pl.BlockSpec(memory_space=pl.ANY)
    full = pl.pallas_call(
        functools.partial(place_kernel, half),
        in_specs=[pl.BlockSpec(memory_space=pltpu.SMEM)] + [anywhere] * 6,
        out_specs=pl.BlockSpec(memory_space=pltpu.VMEM),
        out_shape=jax.ShapeDtypeStruct((n_group * rows, columns), shard.dtype),
        scratch_shapes=[pltpu.SemaphoreType.DMA((6,))],
    )(place, shard, near, far, own_c, near_c, far_c)
    return full


def gather_vectors(members, *gates):
    n_group = lax.axis_size("fsdp")
    f = lax.axis_index("fsdp")
    size = members[0].shape[0]
    rows = [row for member in members for row in member.reshape(-1, size)]
    spot = lax.broadcasted_iota(jnp.int32, (padded(len(rows), 16), size), 0)
    packed = jnp.zeros(spot.shape, bf16)
    for at, row in enumerate(rows):
        packed = jnp.where(spot == at, row[None, :], packed)
    packed = after(packed, *gates)[None]
    pair = lax.ppermute(packed, "fsdp", bit_pairs(n_group, 1))
    both = jnp.concatenate([packed, pair], 0)
    core = lax.ppermute(both, "fsdp", bit_pairs(n_group, 0))
    found = [both[0], core[0], both[1], core[1]]
    ordered = jnp.stack(
        [
            sum(
                jnp.where((f ^ at) == away, found[away], jnp.zeros_like(found[away]))
                for away in range(n_group)
            )
            for at in range(n_group)
        ]
    ).astype(f32)
    outs, start = [], 0
    for member in members:
        count = member.shape[0] // size
        outs.append(ordered[:, start : start + count].reshape(-1))
        start += count
    return outs


def shards(
    inputs,
    skip_input,
    cotangent,
    row_item,
    row_live,
    skip_weight,
    skip_bias,
    attn_gain,
    attn_shift,
    qkv_weight,
    proj_weight,
    proj_bias,
    mlp_gain,
    mlp_shift,
    hidden_weight,
    hidden_bias,
    output_weight,
    output_bias,
):
    model_width = inputs.shape[1]
    skip_start = gather_start(skip_weight)
    skip_full = gather_finish(skip_start)
    (
        skip_vec,
        gain_first,
        shift_first,
        proj_vec,
        gain_second,
        shift_second,
        hidden_vec,
        output_vec,
    ) = gather_vectors(
        [
            skip_bias,
            attn_gain,
            attn_shift,
            proj_bias,
            mlp_gain,
            mlp_shift,
            hidden_bias,
            output_bias,
        ],
    )
    qkv_start = gather_start(qkv_weight, skip_start[1])
    qkv_full = gather_finish(qkv_start)
    proj_start = gather_start(proj_weight, qkv_start[1])
    hidden_start = gather_start(hidden_weight, qkv_start[1])
    output_start = gather_start(output_weight, qkv_start[1])
    joined = jnp.concatenate([inputs, skip_input], axis=1)
    stream_a = times_t(joined, skip_full) + skip_vec
    normed_a = layer_norm(stream_a, gain_first, shift_first).astype(jnp.bfloat16)
    packed = times_t(normed_a, qkv_full).astype(jnp.bfloat16)
    proj_full = gather_finish(proj_start, packed)
    hidden_full = gather_finish(hidden_start, packed)
    output_full = gather_finish(output_start, packed)
    qmark, kmark = marks(row_item, row_live)
    attended, qaug = attention_forward(packed, qmark, kmark)
    stream_b = stream_a + times_t(attended, proj_full) + proj_vec
    normed_b = layer_norm(stream_b, gain_second, shift_second).astype(jnp.bfloat16)
    activation, gelu_slope = hidden_forward(normed_b, hidden_full, hidden_vec)
    grad_out = cotangent * row_live[:, None].astype(jnp.bfloat16)
    grad_output_weight = rows_outer(grad_out, activation).astype(bf16)
    reduce_out = Reducer(grad_output_weight)
    sent = reduce_out.step()
    grad_act = times_n(after(grad_out, sent), output_full)
    grad_pre = (grad_act * gelu_slope.astype(f32)).astype(bf16)
    sent = reduce_out.step(grad_pre)
    grad_hidden_weight = rows_outer(after(grad_pre, sent), normed_b).astype(bf16)
    grad_hidden_bias = column_sums(grad_pre)
    grad_normed_b = times_n(after(grad_pre, grad_hidden_weight), hidden_full)
    _, norm_back = jax.vjp(layer_norm, stream_b, gain_second, shift_second)
    grad_part_b, grad_mlp_gain, grad_mlp_shift = norm_back(grad_normed_b)
    grad_stream_b = grad_out.astype(jnp.float32) + grad_part_b
    grad_branch = grad_stream_b.astype(jnp.bfloat16)
    grad_proj_weight = rows_outer(grad_branch, attended).astype(bf16)
    grad_proj_bias = column_sums(grad_branch)
    grad_attended = times_n(grad_branch, proj_full).astype(jnp.bfloat16)
    reduce_mlp = Reducer(grad_hidden_weight, grad_proj_weight)
    sent = [
        reduce_mlp.step(),
        reduce_out.step(grad_attended),
        reduce_mlp.step(grad_attended),
    ]
    pairs = model_width // LANES
    cuts = [pairs * third // 3 for third in range(4)]
    grad_qkv = None
    for third in range(3):
        grad_qkv = attention_backward(
            packed, after(grad_attended, *sent), attended, qaug, kmark,
            cuts[third], cuts[third + 1] - cuts[third], grad_qkv,
        )
        sent = [reduce_out.step(grad_qkv)]
        if third > 0:
            sent.append(reduce_mlp.step(grad_qkv))
    grad_qkv_weight = rows_outer(after(grad_qkv, sent), normed_a).astype(bf16)
    reduce_qkv = Reducer(grad_qkv_weight)
    sent = [
        reduce_qkv.step(),
        reduce_mlp.step(grad_qkv_weight),
        reduce_out.step(grad_qkv_weight),
    ]
    grad_normed_a = times_n(after(grad_qkv, *sent), qkv_full)
    sent = [
        reduce_qkv.step(grad_normed_a),
    ]
    _, first_back = jax.vjp(layer_norm, stream_a, gain_first, shift_first)
    grad_part_a, grad_attn_gain, grad_attn_shift = first_back(after(grad_normed_a, *sent))
    grad_rounded = (grad_stream_b + grad_part_a).astype(jnp.bfloat16)
    sent = reduce_mlp.step(grad_rounded)
    grad_skip_weight = rows_outer(after(grad_rounded, sent), joined)
    grad_skip_bias = column_sums(grad_rounded)
    grad_output_bias = column_sums(grad_out)
    n_group = lax.axis_size("fsdp")
    rows = model_width // n_group
    vectors = jnp.stack(
        [
            grad_skip_bias,
            grad_attn_gain,
            grad_attn_shift,
            grad_proj_bias,
            grad_mlp_gain,
            grad_mlp_shift,
            grad_output_bias,
        ]
    )
    wide = grad_hidden_bias.reshape(n_group, -1, rows)
    wide_count = wide.shape[1]
    wide = jnp.swapaxes(wide, 0, 1).reshape(wide_count, model_width)
    vectors = jnp.concatenate([vectors, wide], 0)
    vectors = jnp.pad(vectors, ((0, LANES - vectors.shape[0]), (0, 0))).T
    last = jnp.concatenate([grad_skip_weight, vectors], 1).astype(jnp.bfloat16)
    reduce_last = Reducer(last)
    sent = [reduce_last.step(), reduce_mlp.step(last)]
    grad_joined = times_n(after(grad_rounded, *sent), skip_full)
    grad_input = grad_joined[:, :model_width].astype(jnp.bfloat16)
    grad_skip = grad_joined[:, model_width:].astype(jnp.bfloat16)
    sent = [
        reduce_last.step(grad_input, grad_skip),
        reduce_mlp.step(grad_input),
        reduce_qkv.step(grad_input),
    ]
    output = (
        stream_b + times_t(after(activation, *sent), output_full) + output_vec
    ).astype(jnp.bfloat16)
    gate = output
    for _ in range(len(reduce_last.plan)):
        gate = after(reduce_qkv.step(gate), reduce_last.step(gate))
    final_output = reduce_out.finish(output)
    both_final = reduce_mlp.finish(output)
    final_hidden = both_final[: hidden_weight.shape[0]]
    final_proj = both_final[hidden_weight.shape[0] :]
    final_qkv = reduce_qkv.finish()
    last = reduce_last.finish()
    final_skip = last[:, : 2 * model_width]
    final_vec = last[:, 2 * model_width :].T
    final_wide = final_vec[7 : 7 + wide_count].reshape(-1)
    return (
        output,
        grad_input,
        grad_skip,
        final_skip,
        final_vec[0],
        final_vec[1],
        final_vec[2],
        final_qkv,
        final_proj,
        final_vec[3],
        final_vec[4],
        final_vec[5],
        final_hidden,
        final_wide,
        final_output,
        final_vec[6],
    )


def solution(mesh):
    in_specs = (
        P(("dp", "fsdp"), None),
        P(("dp", "fsdp"), None),
        P(("dp", "fsdp"), None),
        P(("dp", "fsdp")),
        P(("dp", "fsdp")),
        P("fsdp", None),
        P("fsdp"),
        P("fsdp"),
        P("fsdp"),
        P("fsdp", None),
        P("fsdp", None),
        P("fsdp"),
        P("fsdp"),
        P("fsdp"),
        P("fsdp", None),
        P("fsdp"),
        P("fsdp", None),
        P("fsdp"),
    )
    out_specs = (
        P(("dp", "fsdp"), None),
        P(("dp", "fsdp"), None),
        P(("dp", "fsdp"), None),
        P("fsdp", None),
        P("fsdp"),
        P("fsdp"),
        P("fsdp"),
        P("fsdp", None),
        P("fsdp", None),
        P("fsdp"),
        P("fsdp"),
        P("fsdp"),
        P("fsdp", None),
        P("fsdp"),
        P("fsdp", None),
        P("fsdp"),
    )

    return jax.shard_map(shards, mesh=mesh, in_specs=in_specs, out_specs=out_specs, check_vma=False)
```
